256 devices in a mesh: ctx: 32 (over z_lo, y, x), head: 8 (over z_hi, core).
Axes of the slice: x: 4, y: 4, z: 8 (z_hi: 4, z_lo: 2; z = z_hi * 2 + z_lo), core: 2. Of those that a mesh axis runs over, the one named last changes fastest.
Arguments:
- queries: bfloat16 [8192, 5120], P('ctx', 'head'), may hold values from -800 to 800
- keys: bfloat16 [8192, 5120], P('ctx', 'head'), may hold values from -800 to 800
- values: bfloat16 [8192, 5120], P('ctx', 'head'), may hold values from -6 to 6
- q_gain: float32 [5120], P('head'), may hold values from 0.6 to 1.5
- k_gain: float32 [5120], P('head'), may hold values from 0.6 to 1.5
- ref_keys: bfloat16 [32768, 5120], P('ctx', 'head'), may hold values from -6 to 6
- ref_values: bfloat16 [32768, 5120], P('ctx', 'head'), may hold values from -6 to 6
- out_weight: bfloat16 [5120, 5120], P('head'), may hold values from -0.078125 to 0.078125
- partners: int32 [32, 2, 12], replicated, may hold values from 0 to 63, as said below
- owners: int32 [2], replicated, may hold values from 0 to 31, as said below
- labels: int32 [64], P('ctx'), may hold values from 0 to 1
Outputs:
- attended: bfloat16 [8192, 5120], P('ctx', 'head')
- mixed: bfloat16 [8192, 5120], P('ctx', 'head')
The draws below stay inside these ranges and needn't reach their ends.
Inputs may be any that keep to these rules, and one draw needn't show every extreme that they name: `partners`: over both persons' lists of one context shard, the blocks of any one shard are named at most 1 times, and the blocks of some shard exactly 1 times. `owners`: the persons' identity shards differ, and one of them is the last shard.
All inputs are finite; a program needn't handle non-finite values.
Results may differ from the reference program's by a relative error of at most 0.018.
Values may be sent and summed in bfloat16 or wider, within the bound.
A program may use at most 128 MiB of HBM per device.

```python
import math
import jax
import jax.numpy as jnp
from jax import lax

D = 5120
HD = 128
BLK = 128
P_SIZE = 12
REF = 1024
PERSONS = 2
TOKENS = 8192
NB = 64
BLK_DEV = 2
CAP = 1
N_CTX = 32


def column_scale(key):
    spread = jnp.exp(jax.random.uniform(jax.random.fold_in(key, 1), (D,), minval=0.0, maxval=math.log(10.0)))
    position = jnp.arange(D, dtype=jnp.float32) / (D - 1)
    trend = 2.0 ** position
    return spread * trend


def raw_field(key, salt):
    sub_key = jax.random.fold_in(key, salt)
    base = jnp.clip(jax.random.normal(jax.random.fold_in(sub_key, 2), (TOKENS, D)), -4.0, 4.0)
    row_scale = jnp.exp(jax.random.uniform(jax.random.fold_in(sub_key, 3), (TOKENS, 1), minval=0.0, maxval=math.log(10.0)))
    return base * row_scale


def draw_queries(key, part):
    shared = jax.random.fold_in(key, 100)
    column = column_scale(shared)
    field = raw_field(key, 200) * column[None, :]
    return field.astype(jnp.bfloat16)


def draw_keys(key, part):
    shared = jax.random.fold_in(key, 100)
    column = column_scale(shared)
    field = raw_field(key, 300) * column[None, :]
    return field.astype(jnp.bfloat16)


def draw_partners(key, part):
    request_count = PERSONS * P_SIZE

    def per_shard(shard_key):
        sources = jnp.tile(jax.random.permutation(jax.random.fold_in(shard_key, 1), N_CTX), CAP)[:request_count]
        picks = jax.random.randint(jax.random.fold_in(shard_key, 2), (request_count,), 0, BLK_DEV)
        chosen = jax.random.permutation(jax.random.fold_in(shard_key, 3), sources * BLK_DEV + picks)
        return chosen.reshape(PERSONS, P_SIZE)
    shard_keys = jax.random.split(jax.random.fold_in(key, 41), N_CTX)
    return jax.vmap(per_shard)(shard_keys).astype(jnp.int32)


def draw_owners(key, part):
    others = jax.random.permutation(jax.random.fold_in(key, 43), N_CTX - 1)[:PERSONS - 1]
    last_shard = jnp.full((1,), N_CTX - 1, dtype=jnp.int32)
    chosen = jnp.concatenate([others.astype(jnp.int32), last_shard])
    return jax.random.permutation(jax.random.fold_in(key, 47), chosen).astype(jnp.int32)


def touch_ends(entries, own_key, low, high):
    longest = entries.shape.index(max(entries.shape))
    spots = []
    for shift in (0, 1):
        where = [jax.random.randint(jax.random.fold_in(own_key, axis), (), 0, length) for axis, length in enumerate(entries.shape)]
        where[longest] = (where[longest] + shift) % entries.shape[longest]
        spots.append(tuple(where))
    return entries.at[spots[0]].set(low).at[spots[1]].set(high)


def shard_levels(stream_key, shape, cuts, least, largest):
    def one(dim, blocks):
        draws = jax.random.uniform(jax.random.fold_in(jax.random.fold_in(stream_key, 6), dim), (blocks,), jnp.float32, least / len(cuts), largest / len(cuts))
        return jnp.repeat(jnp.exp(draws), shape[dim] // blocks).reshape((-1,) + (1,) * (len(shape) - dim - 1))

    level = one(*cuts[0])
    for cut in cuts[1:]:
        level = level * one(*cut)
    return level


def centred(rng, extent, scale, bound, pieces=(), kind=jnp.bfloat16):
    values = scale * jax.random.normal(rng, extent, jnp.float32)
    if pieces:
        values = values * shard_levels(rng, extent, pieces, -0.22, 0.18)
    return jnp.clip(values, -bound, bound).astype(kind)


def setup_inputs(seed: int = 0) -> dict:
    seeds = jax.random.split(jax.random.key(seed), 12)
    queries = draw_queries(jax.random.fold_in(seeds[11], 71), 0)
    keys = draw_keys(jax.random.fold_in(seeds[11], 71), 0)
    values = centred(seeds[2], (TOKENS, D), 1.0, 6.0, ((0, 32), (1, 8)))
    q_gain = jnp.clip(jnp.exp(math.log(1.5) - 0.9162907 * jax.random.uniform(seeds[3], (D,), jnp.float32) ** shard_levels(seeds[3], (D,), ((0, 8),), -0.2, 0.2)), 0.6, 1.5)
    k_gain = jnp.clip(jnp.exp(math.log(1.5) - 0.9162907 * jax.random.uniform(seeds[4], (D,), jnp.float32) ** shard_levels(seeds[4], (D,), ((0, 8),), -0.2, 0.2)), 0.6, 1.5)
    ref_keys = centred(seeds[5], (N_CTX * REF, D), 1.0, 6.0, ((0, 32), (1, 8)))
    ref_values = centred(seeds[6], (N_CTX * REF, D), 1.0, 6.0, ((0, 32), (1, 8)))
    out_weight = centred(seeds[7], (D, D), D ** -0.5, 0.078125, ((0, 8),))
    partners = draw_partners(jax.random.fold_in(seeds[11], 71), 0)
    owners = draw_owners(jax.random.fold_in(seeds[11], 71), 0)
    labels = touch_ends(jax.random.randint(seeds[10], (NB,), 0, PERSONS), jax.random.fold_in(seeds[10], 1), 0, PERSONS - 1).astype(jnp.int32)
    return dict(queries=queries, keys=keys, values=values, q_gain=q_gain, k_gain=k_gain, ref_keys=ref_keys, ref_values=ref_values, out_weight=out_weight, partners=partners, owners=owners, labels=labels)


epsilon = 1e-06

def normalize(features, scale_gain, square_total):
    factor = lax.rsqrt(square_total / D + epsilon)
    return (features * factor[:, None] * scale_gain[None, :]).astype(jnp.bfloat16)

def attend_block(query, own_keys, own_values, far_keys, far_values, bank_keys, bank_values):
    row_count, width = query.shape
    head_count = width // HD
    key_set = jnp.concatenate([own_keys, far_keys, bank_keys], axis=0)
    value_set = jnp.concatenate([own_values, far_values, bank_values], axis=0)
    query_heads = query.astype(jnp.float32).reshape(row_count, head_count, HD)
    key_heads = key_set.astype(jnp.float32).reshape(-1, head_count, HD)
    value_heads = value_set.astype(jnp.float32).reshape(-1, head_count, HD)
    scores = jnp.einsum('qhd,khd->hqk', query_heads, key_heads) * HD ** (-0.5)
    row_peak = lax.optimization_barrier(jnp.max(scores, axis=2, keepdims=True))
    exponent = jnp.exp(scores - row_peak)
    denominator = lax.optimization_barrier(jnp.sum(exponent, axis=2))
    weights = lax.optimization_barrier(exponent.astype(jnp.bfloat16))
    combined = jnp.einsum('hqk,khd->qhd', weights.astype(jnp.float32), value_heads)
    return (combined / denominator.T[:, :, None]).reshape(row_count, width).astype(jnp.bfloat16)

def reference(queries, keys, values, q_gain, k_gain, ref_keys, ref_values, out_weight, partners, owners, labels):
    q_float = queries.astype(jnp.float32)
    k_float = keys.astype(jnp.float32)
    q_norm = normalize(q_float, q_gain, lax.optimization_barrier(jnp.sum(q_float * q_float, axis=1)))
    k_norm = normalize(k_float, k_gain, lax.optimization_barrier(jnp.sum(k_float * k_float, axis=1)))
    query_blocks = q_norm.reshape(NB, BLK, D)
    key_blocks = k_norm.reshape(NB, BLK, D)
    value_blocks = values.reshape(NB, BLK, D)
    bank_keys = ref_keys.reshape(N_CTX, REF, D)
    bank_values = ref_values.reshape(N_CTX, REF, D)

    def one_block(position):
        person_label = labels[position]
        shard_index = position // BLK_DEV
        wanted = partners[shard_index, person_label]
        far_keys = key_blocks[wanted].reshape(P_SIZE * BLK, D)
        far_values = value_blocks[wanted].reshape(P_SIZE * BLK, D)
        owner_index = owners[person_label]
        return attend_block(query_blocks[position], key_blocks[position], value_blocks[position], far_keys, far_values, bank_keys[owner_index], bank_values[owner_index])
    attended = lax.map(one_block, jnp.arange(NB, dtype=jnp.int32)).reshape(TOKENS, D)
    mixed = jnp.dot(attended, out_weight, preferred_element_type=jnp.float32).astype(jnp.bfloat16)
    return (attended, mixed)
```

```python
import jax
import jax.numpy as jnp
from jax import lax
from jax.sharding import PartitionSpec as P

D = 5120
HD = 128
BLK = 128


epsilon = 1e-06


def normalize(features, scale_gain, square_total):
    factor = lax.rsqrt(square_total / D + epsilon)
    return (features * factor[:, None] * scale_gain[None, :]).astype(jnp.bfloat16)


def attend_block(query, own_keys, own_values, far_keys, far_values, bank_keys, bank_values):
    row_count, width = query.shape
    head_count = width // HD
    key_set = jnp.concatenate([own_keys, far_keys, bank_keys], axis=0)
    value_set = jnp.concatenate([own_values, far_values, bank_values], axis=0)
    query_heads = query.reshape(row_count, head_count, HD)
    key_heads = key_set.reshape(-1, head_count, HD)
    value_heads = value_set.reshape(-1, head_count, HD)
    scores = jnp.einsum(
        "qhd,khd->hqk", query_heads, key_heads, preferred_element_type=jnp.float32
    ) * HD ** (-0.5)
    row_peak = jnp.max(scores, axis=2, keepdims=True)
    exponent = jnp.exp(scores - row_peak)
    denominator = jnp.sum(exponent, axis=2)
    weights = exponent.astype(jnp.bfloat16)
    combined = jnp.einsum("hqk,khd->qhd", weights, value_heads, preferred_element_type=jnp.float32)
    return (combined / denominator.T[:, :, None]).reshape(row_count, width).astype(jnp.bfloat16)


def shards(
    queries,
    keys,
    values,
    q_gain,
    k_gain,
    ref_keys,
    ref_values,
    out_weight,
    partners,
    owners,
    labels,
):
    tokens, width = queries.shape
    blocks = tokens // BLK
    n_ctx = partners.shape[0]
    persons = partners.shape[1]
    bank_rows = ref_keys.shape[0]
    piece = bank_rows // n_ctx
    own_index = lax.axis_index("ctx")
    q_float = queries.astype(jnp.float32)
    k_float = keys.astype(jnp.float32)
    q_total, k_total = lax.psum(
        (jnp.sum(q_float * q_float, axis=1), jnp.sum(k_float * k_float, axis=1)), "head"
    )
    q_norm = normalize(q_float, q_gain, q_total)
    k_norm = normalize(k_float, k_gain, k_total)
    query_blocks = q_norm.reshape(blocks, BLK, width)
    key_blocks = k_norm.reshape(blocks, BLK, width)
    value_blocks = values.reshape(blocks, BLK, width)

    flat = partners.reshape(n_ctx, -1)
    hit = (flat // blocks) == own_index
    pick = jnp.sum(jnp.where(hit, flat % blocks, 0), axis=1)
    kv_blocks = jnp.stack([key_blocks, value_blocks], axis=1)
    send_blocks = kv_blocks[pick]
    bank = jnp.stack([ref_keys, ref_values]).reshape(2, n_ctx, piece, width)
    send_bank = jnp.transpose(bank, (1, 0, 2, 3))
    send = jnp.concatenate([send_blocks, send_bank], axis=2)
    got = lax.all_to_all(send, "ctx", 0, 0, tiled=True)
    got_blocks = got[:, :, :BLK]
    got_bank = got[:, :, BLK:]

    wanted = partners[own_index]
    far = got_blocks[wanted // blocks]
    far = far.transpose(0, 2, 1, 3, 4).reshape(persons, 2, -1, width)
    mine = got_bank[owners]
    identity = jnp.transpose(lax.all_gather(mine, "ctx", axis=0, tiled=False), (1, 2, 0, 3, 4)).reshape(
        persons, 2, bank_rows, width
    )

    def one_block(position):
        person_label = labels[position]
        return attend_block(
            query_blocks[position],
            key_blocks[position],
            value_blocks[position],
            far[person_label, 0],
            far[person_label, 1],
            identity[person_label, 0],
            identity[person_label, 1],
        )

    attended = lax.map(one_block, jnp.arange(blocks)).reshape(tokens, width)
    partial_out = jnp.dot(attended, out_weight, preferred_element_type=jnp.float32)
    mixed = lax.psum_scatter(
        partial_out.astype(jnp.bfloat16), "head", scatter_dimension=1, tiled=True
    )
    return (attended, mixed)


def solution(mesh):
    return jax.shard_map(
        shards,
        mesh=mesh,
        in_specs=(
            P("ctx", "head"),
            P("ctx", "head"),
            P("ctx", "head"),
            P("head"),
            P("head"),
            P("ctx", "head"),
            P("ctx", "head"),
            P("head", None),
            P(),
            P(),
            P("ctx"),
        ),
        out_specs=(P("ctx", "head"), P("ctx", "head")),
        check_vma=False,
    )
```

```python
import functools

import jax
import jax.numpy as jnp
from jax import lax
from jax.experimental import pallas as pl
from jax.experimental.pallas import tpu as pltpu
from jax.sharding import PartitionSpec as P

MESH = pl.DeviceIdType.MESH

D = 5120
HD = 128
BLK = 128


epsilon = 1e-06


def gather_kernel(axis, other_axis, n, piece_ref, out_ref, send_sem, recv_sem, local_sem):
    me = lax.axis_index(axis)
    other = lax.axis_index(other_axis)

    def device(j):
        return (j, other) if axis == "ctx" else (other, j)

    barrier = pltpu.get_barrier_semaphore()
    for k in range(1, n):
        pl.semaphore_signal(barrier, inc=1, device_id=device(lax.rem(me + k, n)), device_id_type=MESH)
    pl.semaphore_wait(barrier, n - 1)
    local = pltpu.make_async_copy(piece_ref, out_ref.at[me], local_sem)
    local.start()
    sends = []
    for k in range(1, n):
        copy = pltpu.make_async_remote_copy(
            src_ref=piece_ref,
            dst_ref=out_ref.at[me],
            send_sem=send_sem.at[k],
            recv_sem=recv_sem.at[k],
            device_id=device(lax.rem(me + k, n)),
            device_id_type=MESH,
        )
        copy.start()
        sends.append(copy)
    local.wait()
    for copy in sends:
        copy.wait_send()
    for k in range(1, n):
        source = lax.rem(me + n - k, n)
        pltpu.make_async_remote_copy(
            src_ref=piece_ref,
            dst_ref=out_ref.at[source],
            send_sem=send_sem.at[k],
            recv_sem=recv_sem.at[k],
            device_id=device(source),
            device_id_type=MESH,
        ).wait_recv()


def gather_all(piece, axis, other_axis, n, collective_id):
    return pl.pallas_call(
        functools.partial(gather_kernel, axis, other_axis, n),
        out_shape=jax.ShapeDtypeStruct((n,) + piece.shape, piece.dtype),
        in_specs=[pl.BlockSpec(memory_space=pl.ANY)],
        out_specs=pl.BlockSpec(memory_space=pl.ANY),
        scratch_shapes=[
            pltpu.SemaphoreType.DMA((n,)),
            pltpu.SemaphoreType.DMA((n,)),
            pltpu.SemaphoreType.DMA(()),
        ],
        compiler_params=pltpu.CompilerParams(collective_id=collective_id, has_side_effects=True),
    )(piece)


def normalize(features, scale_gain, square_total):
    factor = lax.rsqrt(square_total / D + epsilon)
    return (features * factor[:, None] * scale_gain[None, :]).astype(jnp.bfloat16)


def attend_block(query, own_keys, own_values, far_keys, far_values, bank_keys, bank_values):
    row_count, width = query.shape
    head_count = width // HD
    key_set = jnp.concatenate([own_keys, far_keys, bank_keys], axis=0)
    value_set = jnp.concatenate([own_values, far_values, bank_values], axis=0)
    query_heads = query.reshape(row_count, head_count, HD)
    key_heads = key_set.reshape(-1, head_count, HD)
    value_heads = value_set.reshape(-1, head_count, HD)
    scores = jnp.einsum(
        "qhd,khd->hqk", query_heads, key_heads, preferred_element_type=jnp.float32
    ) * HD ** (-0.5)
    row_peak = jnp.max(scores, axis=2, keepdims=True)
    exponent = jnp.exp(scores - row_peak)
    denominator = jnp.sum(exponent, axis=2)
    weights = exponent.astype(jnp.bfloat16)
    combined = jnp.einsum("hqk,khd->qhd", weights, value_heads, preferred_element_type=jnp.float32)
    return (combined / denominator.T[:, :, None]).reshape(row_count, width).astype(jnp.bfloat16)


def shards(
    queries,
    keys,
    values,
    q_gain,
    k_gain,
    ref_keys,
    ref_values,
    out_weight,
    partners,
    owners,
    labels,
):
    tokens, width = queries.shape
    blocks = tokens // BLK
    n_ctx = partners.shape[0]
    persons = partners.shape[1]
    bank_rows = ref_keys.shape[0]
    piece = bank_rows // n_ctx
    own_index = lax.axis_index("ctx")
    q_float = queries.astype(jnp.float32)
    k_float = keys.astype(jnp.float32)
    n_head = lax.axis_size("head")
    squares = jnp.stack([jnp.sum(q_float * q_float, axis=1), jnp.sum(k_float * k_float, axis=1)])
    q_total, k_total = jnp.sum(gather_all(squares, "head", "ctx", n_head, 1), axis=0)
    q_norm = normalize(q_float, q_gain, q_total)
    k_norm = normalize(k_float, k_gain, k_total)
    query_blocks = q_norm.reshape(blocks, BLK, width)
    key_blocks = k_norm.reshape(blocks, BLK, width)
    value_blocks = values.reshape(blocks, BLK, width)

    flat = partners.reshape(n_ctx, -1)
    hit = (flat // blocks) == own_index
    pick = jnp.sum(jnp.where(hit, flat % blocks, 0), axis=1)
    kv_blocks = jnp.stack([key_blocks, value_blocks], axis=1)
    send_blocks = kv_blocks[pick]
    bank = jnp.stack([ref_keys, ref_values]).reshape(2, n_ctx, piece, width)
    send_bank = jnp.transpose(bank, (1, 0, 2, 3))
    send = jnp.concatenate([send_blocks, send_bank], axis=2)
    got = lax.all_to_all(send, "ctx", 0, 0, tiled=True)
    got_blocks = got[:, :, :BLK]
    got_bank = got[:, :, BLK:]

    wanted = partners[own_index]
    far = got_blocks[wanted // blocks]
    far = far.transpose(0, 2, 1, 3, 4).reshape(persons, 2, -1, width)
    mine = got_bank[owners]
    whole = gather_all(mine.reshape(-1, width), "ctx", "head", n_ctx, 2)
    identity = jnp.transpose(whole.reshape((n_ctx,) + mine.shape), (1, 2, 0, 3, 4)).reshape(
        persons, 2, bank_rows, width
    )

    def one_block(position):
        person_label = labels[position]
        return attend_block(
            query_blocks[position],
            key_blocks[position],
            value_blocks[position],
            far[person_label, 0],
            far[person_label, 1],
            identity[person_label, 0],
            identity[person_label, 1],
        )

    attended = lax.map(one_block, jnp.arange(blocks)).reshape(tokens, width)
    partial_out = jnp.dot(attended, out_weight, preferred_element_type=jnp.float32)
    mixed = lax.psum_scatter(
        partial_out.astype(jnp.bfloat16), "head", scatter_dimension=1, tiled=True
    )
    return (attended, mixed)


def solution(mesh):
    return jax.shard_map(
        shards,
        mesh=mesh,
        in_specs=(
            P("ctx", "head"),
            P("ctx", "head"),
            P("ctx", "head"),
            P("head"),
            P("head"),
            P("ctx", "head"),
            P("ctx", "head"),
            P("head", None),
            P(),
            P(),
            P("ctx"),
        ),
        out_specs=(P("ctx", "head"), P("ctx", "head")),
        check_vma=False,
    )
```

```python
import functools

import jax
import jax.numpy as jnp
from jax import lax
from jax.experimental import pallas as pl
from jax.experimental.pallas import tpu as pltpu
from jax.sharding import PartitionSpec as P

MESH = pl.DeviceIdType.MESH

D = 5120
HD = 128
BLK = 128


epsilon = 1e-06


def gather_kernel(axis, other_axis, n, piece_ref, out_ref, send_sem, recv_sem, local_sem):
    me = lax.axis_index(axis)
    other = lax.axis_index(other_axis)

    def device(j):
        return (j, other) if axis == "ctx" else (other, j)

    barrier = pltpu.get_barrier_semaphore()
    for k in range(1, n):
        pl.semaphore_signal(barrier, inc=1, device_id=device(lax.rem(me + k, n)), device_id_type=MESH)
    pl.semaphore_wait(barrier, n - 1)
    local = pltpu.make_async_copy(piece_ref, out_ref.at[me], local_sem)
    local.start()
    sends = []
    for k in range(1, n):
        copy = pltpu.make_async_remote_copy(
            src_ref=piece_ref,
            dst_ref=out_ref.at[me],
            send_sem=send_sem.at[k],
            recv_sem=recv_sem.at[k],
            device_id=device(lax.rem(me + k, n)),
            device_id_type=MESH,
        )
        copy.start()
        sends.append(copy)
    local.wait()
    for copy in sends:
        copy.wait_send()
    for k in range(1, n):
        source = lax.rem(me + n - k, n)
        pltpu.make_async_remote_copy(
            src_ref=piece_ref,
            dst_ref=out_ref.at[source],
            send_sem=send_sem.at[k],
            recv_sem=recv_sem.at[k],
            device_id=device(source),
            device_id_type=MESH,
        ).wait_recv()


def gather_all(piece, axis, other_axis, n, collective_id):
    return pl.pallas_call(
        functools.partial(gather_kernel, axis, other_axis, n),
        out_shape=jax.ShapeDtypeStruct((n,) + piece.shape, piece.dtype),
        in_specs=[pl.BlockSpec(memory_space=pl.ANY)],
        out_specs=pl.BlockSpec(memory_space=pl.ANY),
        scratch_shapes=[
            pltpu.SemaphoreType.DMA((n,)),
            pltpu.SemaphoreType.DMA((n,)),
            pltpu.SemaphoreType.DMA(()),
        ],
        compiler_params=pltpu.CompilerParams(collective_id=collective_id, has_side_effects=True),
    )(piece)


def attend_kernel(
    label_ref, source_ref, q_ref, k_ref, v_ref, got_ref, whole_ref, o_ref,
    far_k, far_v, bank_k, bank_v, sem_k, sem_v, sem_bank,
):
    position = pl.program_id(0)
    person = label_ref[position]
    far_count = far_k.shape[0] // BLK
    piece = bank_k.shape[1]
    copies = []
    for j in range(far_count):
        source = source_ref[person * far_count + j]
        copies.append(pltpu.make_async_copy(
            got_ref.at[source, 0, pl.ds(0, BLK)], far_k.at[pl.ds(j * BLK, BLK)], sem_k.at[j]))
        copies.append(pltpu.make_async_copy(
            got_ref.at[source, 1, pl.ds(0, BLK)], far_v.at[pl.ds(j * BLK, BLK)], sem_v.at[j]))
    copies.append(pltpu.make_async_copy(
        whole_ref.at[:, pl.ds(person * 2 * piece, piece)], bank_k, sem_bank.at[0]))
    copies.append(pltpu.make_async_copy(
        whole_ref.at[:, pl.ds(person * 2 * piece + piece, piece)], bank_v, sem_bank.at[1]))
    for copy in copies:
        copy.start()
    for copy in copies:
        copy.wait()
    rows, width = q_ref.shape
    bank_rows = bank_k.shape[0] * piece
    dims = (((1,), (1,)), ((), ()))
    for h in range(width // HD):
        cols = pl.ds(h * HD, HD)
        query = q_ref[:, cols]
        parts = [
            (k_ref[:, cols], v_ref[:, cols]),
            (far_k[:, cols], far_v[:, cols]),
            (bank_k[:, :, cols].reshape(bank_rows, HD), bank_v[:, :, cols].reshape(bank_rows, HD)),
        ]
        scores = [
            lax.dot_general(query, key, dims, preferred_element_type=jnp.float32) * HD ** (-0.5)
            for key, _ in parts
        ]
        peak = jnp.max(scores[0], axis=1, keepdims=True)
        for score in scores[1:]:
            peak = jnp.maximum(peak, jnp.max(score, axis=1, keepdims=True))
        total = None
        summed = None
        for score, (_, value) in zip(scores, parts):
            exponent = jnp.exp(score - peak)
            part_sum = jnp.sum(exponent, axis=1, keepdims=True)
            product = jnp.dot(exponent.astype(jnp.bfloat16), value, preferred_element_type=jnp.float32)
            total = part_sum if total is None else total + part_sum
            summed = product if summed is None else summed + product
        o_ref[:, cols] = (summed / total).astype(o_ref.dtype)


def attend(labels, sources, q_norm, k_norm, values, got, whole, n_ctx, far_count):
    rows, width = q_norm.shape
    piece = whole.shape[1] // 4
    block = pl.BlockSpec((BLK, width), lambda b, lab, src: (b, 0))
    return pl.pallas_call(
        attend_kernel,
        out_shape=jax.ShapeDtypeStruct((rows, width), jnp.bfloat16),
        grid_spec=pltpu.PrefetchScalarGridSpec(
            num_scalar_prefetch=2,
            grid=(rows // BLK,),
            in_specs=[block, block, block, pl.BlockSpec(memory_space=pl.ANY), pl.BlockSpec(memory_space=pl.ANY)],
            out_specs=block,
            scratch_shapes=[
                pltpu.VMEM((far_count * BLK, width), jnp.bfloat16),
                pltpu.VMEM((far_count * BLK, width), jnp.bfloat16),
                pltpu.VMEM((n_ctx, piece, width), jnp.bfloat16),
                pltpu.VMEM((n_ctx, piece, width), jnp.bfloat16),
                pltpu.SemaphoreType.DMA((far_count,)),
                pltpu.SemaphoreType.DMA((far_count,)),
                pltpu.SemaphoreType.DMA((2,)),
            ],
        ),
        compiler_params=pltpu.CompilerParams(dimension_semantics=("arbitrary",)),
    )(labels, sources, q_norm, k_norm, values, got, whole)


def normalize(features, scale_gain, square_total):
    factor = lax.rsqrt(square_total / D + epsilon)
    return (features * factor[:, None] * scale_gain[None, :]).astype(jnp.bfloat16)


def attend_block(query, own_keys, own_values, far_keys, far_values, bank_keys, bank_values):
    row_count, width = query.shape
    head_count = width // HD
    key_set = jnp.concatenate([own_keys, far_keys, bank_keys], axis=0)
    value_set = jnp.concatenate([own_values, far_values, bank_values], axis=0)
    query_heads = query.reshape(row_count, head_count, HD)
    key_heads = key_set.reshape(-1, head_count, HD)
    value_heads = value_set.reshape(-1, head_count, HD)
    scores = jnp.einsum(
        "qhd,khd->hqk", query_heads, key_heads, preferred_element_type=jnp.float32
    ) * HD ** (-0.5)
    row_peak = jnp.max(scores, axis=2, keepdims=True)
    exponent = jnp.exp(scores - row_peak)
    denominator = jnp.sum(exponent, axis=2)
    weights = exponent.astype(jnp.bfloat16)
    combined = jnp.einsum("hqk,khd->qhd", weights, value_heads, preferred_element_type=jnp.float32)
    return (combined / denominator.T[:, :, None]).reshape(row_count, width).astype(jnp.bfloat16)


def shards(
    queries,
    keys,
    values,
    q_gain,
    k_gain,
    ref_keys,
    ref_values,
    out_weight,
    partners,
    owners,
    labels,
):
    tokens, width = queries.shape
    blocks = tokens // BLK
    n_ctx = partners.shape[0]
    persons = partners.shape[1]
    bank_rows = ref_keys.shape[0]
    piece = bank_rows // n_ctx
    own_index = lax.axis_index("ctx")
    q_float = queries.astype(jnp.float32)
    k_float = keys.astype(jnp.float32)
    n_head = lax.axis_size("head")
    squares = jnp.stack([jnp.sum(q_float * q_float, axis=1), jnp.sum(k_float * k_float, axis=1)])
    q_total, k_total = jnp.sum(gather_all(squares, "head", "ctx", n_head, 1), axis=0)
    q_norm = normalize(q_float, q_gain, q_total)
    k_norm = normalize(k_float, k_gain, k_total)
    query_blocks = q_norm.reshape(blocks, BLK, width)
    key_blocks = k_norm.reshape(blocks, BLK, width)
    value_blocks = values.reshape(blocks, BLK, width)

    flat = partners.reshape(n_ctx, -1)
    hit = (flat // blocks) == own_index
    pick = jnp.sum(jnp.where(hit, flat % blocks, 0), axis=1)
    kv_blocks = jnp.stack([key_blocks, value_blocks], axis=1)
    send_blocks = kv_blocks[pick]
    bank = jnp.stack([ref_keys, ref_values]).reshape(2, n_ctx, piece, width)
    send_bank = jnp.transpose(bank, (1, 0, 2, 3))
    send = jnp.concatenate([send_blocks, send_bank], axis=2)
    got = lax.all_to_all(send, "ctx", 0, 0, tiled=True)
    got_bank = got[:, :, BLK:]

    sources = (partners[own_index] // blocks).reshape(-1)
    mine = got_bank[owners]
    whole = gather_all(mine.reshape(-1, width), "ctx", "head", n_ctx, 2)
    attended = attend(labels, sources, q_norm, k_norm, values, got, whole, n_ctx, partners.shape[2])
    partial_out = jnp.dot(attended, out_weight, preferred_element_type=jnp.float32)
    mixed = lax.psum_scatter(
        partial_out.astype(jnp.bfloat16), "head", scatter_dimension=1, tiled=True
    )
    return (attended, mixed)


def solution(mesh):
    return jax.shard_map(
        shards,
        mesh=mesh,
        in_specs=(
            P("ctx", "head"),
            P("ctx", "head"),
            P("ctx", "head"),
            P("head"),
            P("head"),
            P("ctx", "head"),
            P("ctx", "head"),
            P("head", None),
            P(),
            P(),
            P("ctx"),
        ),
        out_specs=(P("ctx", "head"), P("ctx", "head")),
        check_vma=False,
    )
```

```python
import functools

import jax
import jax.numpy as jnp
from jax import lax
from jax.experimental import pallas as pl
from jax.experimental.pallas import tpu as pltpu
from jax.sharding import PartitionSpec as P

MESH = pl.DeviceIdType.MESH

D = 5120
HD = 128
BLK = 128


epsilon = 1e-06


def gather_kernel(axis, other_axis, n, piece_ref, out_ref, send_sem, recv_sem, local_sem):
    me = lax.axis_index(axis)
    other = lax.axis_index(other_axis)

    def device(j):
        return (j, other) if axis == "ctx" else (other, j)

    barrier = pltpu.get_barrier_semaphore()
    for k in range(1, n):
        pl.semaphore_signal(barrier, inc=1, device_id=device(lax.rem(me + k, n)), device_id_type=MESH)
    pl.semaphore_wait(barrier, n - 1)
    local = pltpu.make_async_copy(piece_ref, out_ref.at[me], local_sem)
    local.start()
    sends = []
    for k in range(1, n):
        copy = pltpu.make_async_remote_copy(
            src_ref=piece_ref,
            dst_ref=out_ref.at[me],
            send_sem=send_sem.at[k],
            recv_sem=recv_sem.at[k],
            device_id=device(lax.rem(me + k, n)),
            device_id_type=MESH,
        )
        copy.start()
        sends.append(copy)
    local.wait()
    for copy in sends:
        copy.wait_send()
    for k in range(1, n):
        source = lax.rem(me + n - k, n)
        pltpu.make_async_remote_copy(
            src_ref=piece_ref,
            dst_ref=out_ref.at[source],
            send_sem=send_sem.at[k],
            recv_sem=recv_sem.at[k],
            device_id=device(source),
            device_id_type=MESH,
        ).wait_recv()


def scatter_kernel(axis, other_axis, n, piece, keys_ref, values_ref, out_ref, send_sem, recv_sem, local_sem):
    me = lax.axis_index(axis)
    other = lax.axis_index(other_axis)

    def device(j):
        return (j, other) if axis == "ctx" else (other, j)

    def rows(j):
        return pl.ds(pl.multiple_of(j * piece, piece), piece)

    barrier = pltpu.get_barrier_semaphore()
    for k in range(1, n):
        pl.semaphore_signal(barrier, inc=1, device_id=device(lax.rem(me + k, n)), device_id_type=MESH)
    pl.semaphore_wait(barrier, n - 1)
    sources = (keys_ref, values_ref)
    local = [
        pltpu.make_async_copy(src.at[rows(me)], out_ref.at[me, t], local_sem.at[t])
        for t, src in enumerate(sources)
    ]
    for copy in local:
        copy.start()
    sends = []
    for k in range(1, n):
        peer = lax.rem(me + k, n)
        for t, src in enumerate(sources):
            copy = pltpu.make_async_remote_copy(
                src_ref=src.at[rows(peer)],
                dst_ref=out_ref.at[me, t],
                send_sem=send_sem.at[k, t],
                recv_sem=recv_sem.at[k, t],
                device_id=device(peer),
                device_id_type=MESH,
            )
            copy.start()
            sends.append(copy)
    for copy in local:
        copy.wait()
    for copy in sends:
        copy.wait_send()
    for k in range(1, n):
        source = lax.rem(me + n - k, n)
        for t, src in enumerate(sources):
            pltpu.make_async_remote_copy(
                src_ref=src.at[rows(me)],
                dst_ref=out_ref.at[source, t],
                send_sem=send_sem.at[k, t],
                recv_sem=recv_sem.at[k, t],
                device_id=device(source),
                device_id_type=MESH,
            ).wait_recv()


def scatter_bank(ref_keys, ref_values, axis, other_axis, n, collective_id):
    rows, width = ref_keys.shape
    piece = rows // n
    return pl.pallas_call(
        functools.partial(scatter_kernel, axis, other_axis, n, piece),
        out_shape=jax.ShapeDtypeStruct((n, 2, piece, width), ref_keys.dtype),
        in_specs=[pl.BlockSpec(memory_space=pl.ANY)] * 2,
        out_specs=pl.BlockSpec(memory_space=pl.ANY),
        scratch_shapes=[
            pltpu.SemaphoreType.DMA((n, 2)),
            pltpu.SemaphoreType.DMA((n, 2)),
            pltpu.SemaphoreType.DMA((2,)),
        ],
        compiler_params=pltpu.CompilerParams(collective_id=collective_id, has_side_effects=True),
    )(ref_keys, ref_values)


def gather_all(piece, axis, other_axis, n, collective_id):
    return pl.pallas_call(
        functools.partial(gather_kernel, axis, other_axis, n),
        out_shape=jax.ShapeDtypeStruct((n,) + piece.shape, piece.dtype),
        in_specs=[pl.BlockSpec(memory_space=pl.ANY)],
        out_specs=pl.BlockSpec(memory_space=pl.ANY),
        scratch_shapes=[
            pltpu.SemaphoreType.DMA((n,)),
            pltpu.SemaphoreType.DMA((n,)),
            pltpu.SemaphoreType.DMA(()),
        ],
        compiler_params=pltpu.CompilerParams(collective_id=collective_id, has_side_effects=True),
    )(piece)


def attend_kernel(
    label_ref, source_ref, q_ref, k_ref, v_ref, got_ref, whole_ref, o_ref,
    far_k, far_v, bank_k, bank_v, sem_k, sem_v, sem_bank,
):
    position = pl.program_id(0)
    person = label_ref[position]
    far_count = far_k.shape[0] // BLK
    piece = bank_k.shape[1]
    copies = []
    for j in range(far_count):
        source = source_ref[person * far_count + j]
        copies.append(pltpu.make_async_copy(
            got_ref.at[source, 0, pl.ds(0, BLK)], far_k.at[pl.ds(j * BLK, BLK)], sem_k.at[j]))
        copies.append(pltpu.make_async_copy(
            got_ref.at[source, 1, pl.ds(0, BLK)], far_v.at[pl.ds(j * BLK, BLK)], sem_v.at[j]))
    copies.append(pltpu.make_async_copy(
        whole_ref.at[:, pl.ds(person * 2 * piece, piece)], bank_k, sem_bank.at[0]))
    copies.append(pltpu.make_async_copy(
        whole_ref.at[:, pl.ds(person * 2 * piece + piece, piece)], bank_v, sem_bank.at[1]))
    for copy in copies:
        copy.start()
    for copy in copies:
        copy.wait()
    rows, width = q_ref.shape
    bank_rows = bank_k.shape[0] * piece
    dims = (((1,), (1,)), ((), ()))
    for h in range(width // HD):
        cols = pl.ds(h * HD, HD)
        query = q_ref[:, cols]
        parts = [
            (k_ref[:, cols], v_ref[:, cols]),
            (far_k[:, cols], far_v[:, cols]),
            (bank_k[:, :, cols].reshape(bank_rows, HD), bank_v[:, :, cols].reshape(bank_rows, HD)),
        ]
        scores = [
            lax.dot_general(query, key, dims, preferred_element_type=jnp.float32) * HD ** (-0.5)
            for key, _ in parts
        ]
        peak = jnp.max(scores[0], axis=1, keepdims=True)
        for score in scores[1:]:
            peak = jnp.maximum(peak, jnp.max(score, axis=1, keepdims=True))
        total = None
        summed = None
        for score, (_, value) in zip(scores, parts):
            exponent = jnp.exp(score - peak)
            part_sum = jnp.sum(exponent, axis=1, keepdims=True)
            product = jnp.dot(exponent.astype(jnp.bfloat16), value, preferred_element_type=jnp.float32)
            total = part_sum if total is None else total + part_sum
            summed = product if summed is None else summed + product
        o_ref[:, cols] = (summed / total).astype(o_ref.dtype)


def attend(labels, sources, q_norm, k_norm, values, got, whole, n_ctx, far_count):
    rows, width = q_norm.shape
    piece = whole.shape[1] // 4
    block = pl.BlockSpec((BLK, width), lambda b, lab, src: (b, 0))
    return pl.pallas_call(
        attend_kernel,
        out_shape=jax.ShapeDtypeStruct((rows, width), jnp.bfloat16),
        grid_spec=pltpu.PrefetchScalarGridSpec(
            num_scalar_prefetch=2,
            grid=(rows // BLK,),
            in_specs=[block, block, block, pl.BlockSpec(memory_space=pl.ANY), pl.BlockSpec(memory_space=pl.ANY)],
            out_specs=block,
            scratch_shapes=[
                pltpu.VMEM((far_count * BLK, width), jnp.bfloat16),
                pltpu.VMEM((far_count * BLK, width), jnp.bfloat16),
                pltpu.VMEM((n_ctx, piece, width), jnp.bfloat16),
                pltpu.VMEM((n_ctx, piece, width), jnp.bfloat16),
                pltpu.SemaphoreType.DMA((far_count,)),
                pltpu.SemaphoreType.DMA((far_count,)),
                pltpu.SemaphoreType.DMA((2,)),
            ],
        ),
        compiler_params=pltpu.CompilerParams(dimension_semantics=("arbitrary",)),
    )(labels, sources, q_norm, k_norm, values, got, whole)


def normalize(features, scale_gain, square_total):
    factor = lax.rsqrt(square_total / D + epsilon)
    return (features * factor[:, None] * scale_gain[None, :]).astype(jnp.bfloat16)


def attend_block(query, own_keys, own_values, far_keys, far_values, bank_keys, bank_values):
    row_count, width = query.shape
    head_count = width // HD
    key_set = jnp.concatenate([own_keys, far_keys, bank_keys], axis=0)
    value_set = jnp.concatenate([own_values, far_values, bank_values], axis=0)
    query_heads = query.reshape(row_count, head_count, HD)
    key_heads = key_set.reshape(-1, head_count, HD)
    value_heads = value_set.reshape(-1, head_count, HD)
    scores = jnp.einsum(
        "qhd,khd->hqk", query_heads, key_heads, preferred_element_type=jnp.float32
    ) * HD ** (-0.5)
    row_peak = jnp.max(scores, axis=2, keepdims=True)
    exponent = jnp.exp(scores - row_peak)
    denominator = jnp.sum(exponent, axis=2)
    weights = exponent.astype(jnp.bfloat16)
    combined = jnp.einsum("hqk,khd->qhd", weights, value_heads, preferred_element_type=jnp.float32)
    return (combined / denominator.T[:, :, None]).reshape(row_count, width).astype(jnp.bfloat16)


def shards(
    queries,
    keys,
    values,
    q_gain,
    k_gain,
    ref_keys,
    ref_values,
    out_weight,
    partners,
    owners,
    labels,
):
    tokens, width = queries.shape
    blocks = tokens // BLK
    n_ctx = partners.shape[0]
    persons = partners.shape[1]
    bank_rows = ref_keys.shape[0]
    piece = bank_rows // n_ctx
    own_index = lax.axis_index("ctx")
    q_float = queries.astype(jnp.float32)
    k_float = keys.astype(jnp.float32)
    n_head = lax.axis_size("head")
    squares = jnp.stack([jnp.sum(q_float * q_float, axis=1), jnp.sum(k_float * k_float, axis=1)])
    q_total, k_total = jnp.sum(gather_all(squares, "head", "ctx", n_head, 1), axis=0)
    q_norm = normalize(q_float, q_gain, q_total)
    k_norm = normalize(k_float, k_gain, k_total)
    query_blocks = q_norm.reshape(blocks, BLK, width)
    key_blocks = k_norm.reshape(blocks, BLK, width)
    value_blocks = values.reshape(blocks, BLK, width)

    flat = partners.reshape(n_ctx, -1)
    hit = (flat // blocks) == own_index
    pick = jnp.sum(jnp.where(hit, flat % blocks, 0), axis=1)
    kv_blocks = jnp.stack([key_blocks, value_blocks], axis=1)
    send = kv_blocks[pick]
    got = lax.all_to_all(send, "ctx", 0, 0, tiled=True)
    got_bank = scatter_bank(ref_keys, ref_values, "ctx", "head", n_ctx, 3)

    sources = (partners[own_index] // blocks).reshape(-1)
    mine = got_bank[owners]
    whole = gather_all(mine.reshape(-1, width), "ctx", "head", n_ctx, 2)
    attended = attend(labels, sources, q_norm, k_norm, values, got, whole, n_ctx, partners.shape[2])
    partial_out = jnp.dot(attended, out_weight, preferred_element_type=jnp.float32)
    mixed = lax.psum_scatter(
        partial_out.astype(jnp.bfloat16), "head", scatter_dimension=1, tiled=True
    )
    return (attended, mixed)


def solution(mesh):
    return jax.shard_map(
        shards,
        mesh=mesh,
        in_specs=(
            P("ctx", "head"),
            P("ctx", "head"),
            P("ctx", "head"),
            P("head"),
            P("head"),
            P("ctx", "head"),
            P("ctx", "head"),
            P("head", None),
            P(),
            P(),
            P("ctx"),
        ),
        out_specs=(P("ctx", "head"), P("ctx", "head")),
        check_vma=False,
    )
```

```python
import functools

import jax
import jax.numpy as jnp
from jax import lax
from jax.experimental import pallas as pl
from jax.experimental.pallas import tpu as pltpu
from jax.sharding import PartitionSpec as P

MESH = pl.DeviceIdType.MESH

D = 5120
HD = 128
BLK = 128


epsilon = 1e-06


def gather_kernel(axis, other_axis, n, piece_ref, out_ref, send_sem, recv_sem, local_sem):
    me = lax.axis_index(axis)
    other = lax.axis_index(other_axis)

    def device(j):
        return (j, other) if axis == "ctx" else (other, j)

    barrier = pltpu.get_barrier_semaphore()
    for k in range(1, n):
        pl.semaphore_signal(barrier, inc=1, device_id=device(lax.rem(me + k, n)), device_id_type=MESH)
    pl.semaphore_wait(barrier, n - 1)
    local = pltpu.make_async_copy(piece_ref, out_ref.at[me], local_sem)
    local.start()
    sends = []
    for k in range(1, n):
        copy = pltpu.make_async_remote_copy(
            src_ref=piece_ref,
            dst_ref=out_ref.at[me],
            send_sem=send_sem.at[k],
            recv_sem=recv_sem.at[k],
            device_id=device(lax.rem(me + k, n)),
            device_id_type=MESH,
        )
        copy.start()
        sends.append(copy)
    local.wait()
    for copy in sends:
        copy.wait_send()
    for k in range(1, n):
        source = lax.rem(me + n - k, n)
        pltpu.make_async_remote_copy(
            src_ref=piece_ref,
            dst_ref=out_ref.at[source],
            send_sem=send_sem.at[k],
            recv_sem=recv_sem.at[k],
            device_id=device(source),
            device_id_type=MESH,
        ).wait_recv()


def scatter_kernel(axis, other_axis, n, piece, keys_ref, values_ref, out_ref, send_sem, recv_sem, local_sem):
    me = lax.axis_index(axis)
    other = lax.axis_index(other_axis)

    def device(j):
        return (j, other) if axis == "ctx" else (other, j)

    def rows(j):
        return pl.ds(pl.multiple_of(j * piece, piece), piece)

    barrier = pltpu.get_barrier_semaphore()
    for k in range(1, n):
        pl.semaphore_signal(barrier, inc=1, device_id=device(lax.rem(me + k, n)), device_id_type=MESH)
    pl.semaphore_wait(barrier, n - 1)
    sources = (keys_ref, values_ref)
    local = [
        pltpu.make_async_copy(src.at[rows(me)], out_ref.at[me, t], local_sem.at[t])
        for t, src in enumerate(sources)
    ]
    for copy in local:
        copy.start()
    sends = []
    for k in range(1, n):
        peer = lax.rem(me + k, n)
        for t, src in enumerate(sources):
            copy = pltpu.make_async_remote_copy(
                src_ref=src.at[rows(peer)],
                dst_ref=out_ref.at[me, t],
                send_sem=send_sem.at[k, t],
                recv_sem=recv_sem.at[k, t],
                device_id=device(peer),
                device_id_type=MESH,
            )
            copy.start()
            sends.append(copy)
    for copy in local:
        copy.wait()
    for copy in sends:
        copy.wait_send()
    for k in range(1, n):
        source = lax.rem(me + n - k, n)
        for t, src in enumerate(sources):
            pltpu.make_async_remote_copy(
                src_ref=src.at[rows(me)],
                dst_ref=out_ref.at[source, t],
                send_sem=send_sem.at[k, t],
                recv_sem=recv_sem.at[k, t],
                device_id=device(source),
                device_id_type=MESH,
            ).wait_recv()


def scatter_bank(ref_keys, ref_values, axis, other_axis, n, collective_id):
    rows, width = ref_keys.shape
    piece = rows // n
    return pl.pallas_call(
        functools.partial(scatter_kernel, axis, other_axis, n, piece),
        out_shape=jax.ShapeDtypeStruct((n, 2, piece, width), ref_keys.dtype),
        in_specs=[pl.BlockSpec(memory_space=pl.ANY)] * 2,
        out_specs=pl.BlockSpec(memory_space=pl.ANY),
        scratch_shapes=[
            pltpu.SemaphoreType.DMA((n, 2)),
            pltpu.SemaphoreType.DMA((n, 2)),
            pltpu.SemaphoreType.DMA((2,)),
        ],
        compiler_params=pltpu.CompilerParams(collective_id=collective_id, has_side_effects=True),
    )(ref_keys, ref_values)


def gather_all(piece, axis, other_axis, n, collective_id):
    return pl.pallas_call(
        functools.partial(gather_kernel, axis, other_axis, n),
        out_shape=jax.ShapeDtypeStruct((n,) + piece.shape, piece.dtype),
        in_specs=[pl.BlockSpec(memory_space=pl.ANY)],
        out_specs=pl.BlockSpec(memory_space=pl.ANY),
        scratch_shapes=[
            pltpu.SemaphoreType.DMA((n,)),
            pltpu.SemaphoreType.DMA((n,)),
            pltpu.SemaphoreType.DMA(()),
        ],
        compiler_params=pltpu.CompilerParams(collective_id=collective_id, has_side_effects=True),
    )(piece)


def attend_kernel(
    label_ref, source_ref, q_ref, k_ref, v_ref, factor_ref, gain_ref, got_ref, whole_ref, o_ref,
    far_k, far_v, bank_k, bank_v, sem_k, sem_v, sem_bank,
):
    position = pl.program_id(0)
    person = label_ref[position]
    far_count = far_k.shape[0] // BLK
    piece = bank_k.shape[1]
    copies = []
    for j in range(far_count):
        source = source_ref[person * far_count + j]
        copies.append(pltpu.make_async_copy(
            got_ref.at[source, 0, pl.ds(0, BLK)], far_k.at[pl.ds(j * BLK, BLK)], sem_k.at[j]))
        copies.append(pltpu.make_async_copy(
            got_ref.at[source, 1, pl.ds(0, BLK)], far_v.at[pl.ds(j * BLK, BLK)], sem_v.at[j]))
    copies.append(pltpu.make_async_copy(
        whole_ref.at[:, pl.ds(person * 2 * piece, piece)], bank_k, sem_bank.at[0]))
    copies.append(pltpu.make_async_copy(
        whole_ref.at[:, pl.ds(person * 2 * piece + piece, piece)], bank_v, sem_bank.at[1]))
    for copy in copies:
        copy.start()
    for copy in copies:
        copy.wait()
    far_k[...] = (far_k[...].astype(jnp.float32) * factor_ref[...] * gain_ref[...]).astype(far_k.dtype)
    rows, width = q_ref.shape
    bank_rows = bank_k.shape[0] * piece
    dims = (((1,), (1,)), ((), ()))
    for h in range(width // HD):
        cols = pl.ds(h * HD, HD)
        query = q_ref[:, cols]
        parts = [
            (k_ref[:, cols], v_ref[:, cols]),
            (far_k[:, cols], far_v[:, cols]),
            (bank_k[:, :, cols].reshape(bank_rows, HD), bank_v[:, :, cols].reshape(bank_rows, HD)),
        ]
        scores = [
            lax.dot_general(query, key, dims, preferred_element_type=jnp.float32) * HD ** (-0.5)
            for key, _ in parts
        ]
        peak = jnp.max(scores[0], axis=1, keepdims=True)
        for score in scores[1:]:
            peak = jnp.maximum(peak, jnp.max(score, axis=1, keepdims=True))
        total = None
        summed = None
        for score, (_, value) in zip(scores, parts):
            exponent = jnp.exp(score - peak)
            part_sum = jnp.sum(exponent, axis=1, keepdims=True)
            product = jnp.dot(exponent.astype(jnp.bfloat16), value, preferred_element_type=jnp.float32)
            total = part_sum if total is None else total + part_sum
            summed = product if summed is None else summed + product
        o_ref[:, cols] = (summed / total).astype(o_ref.dtype)


def attend(labels, sources, q_norm, k_norm, values, far_factor, k_gain, got, whole, n_ctx, far_count):
    rows, width = q_norm.shape
    piece = whole.shape[1] // 4
    block = pl.BlockSpec((BLK, width), lambda b, lab, src: (b, 0))
    return pl.pallas_call(
        attend_kernel,
        out_shape=jax.ShapeDtypeStruct((rows, width), jnp.bfloat16),
        grid_spec=pltpu.PrefetchScalarGridSpec(
            num_scalar_prefetch=2,
            grid=(rows // BLK,),
            in_specs=[
                block,
                block,
                block,
                pl.BlockSpec((None, far_count * BLK, 1), lambda b, lab, src: (lab[b], 0, 0)),
                pl.BlockSpec((1, width), lambda b, lab, src: (0, 0)),
                pl.BlockSpec(memory_space=pl.ANY),
                pl.BlockSpec(memory_space=pl.ANY),
            ],
            out_specs=block,
            scratch_shapes=[
                pltpu.VMEM((far_count * BLK, width), jnp.bfloat16),
                pltpu.VMEM((far_count * BLK, width), jnp.bfloat16),
                pltpu.VMEM((n_ctx, piece, width), jnp.bfloat16),
                pltpu.VMEM((n_ctx, piece, width), jnp.bfloat16),
                pltpu.SemaphoreType.DMA((far_count,)),
                pltpu.SemaphoreType.DMA((far_count,)),
                pltpu.SemaphoreType.DMA((2,)),
            ],
        ),
        compiler_params=pltpu.CompilerParams(dimension_semantics=("arbitrary",)),
    )(labels, sources, q_norm, k_norm, values, far_factor, k_gain.reshape(1, width), got, whole)


def normalize(features, scale_gain, square_total):
    factor = lax.rsqrt(square_total / D + epsilon)
    return (features * factor[:, None] * scale_gain[None, :]).astype(jnp.bfloat16)


def attend_block(query, own_keys, own_values, far_keys, far_values, bank_keys, bank_values):
    row_count, width = query.shape
    head_count = width // HD
    key_set = jnp.concatenate([own_keys, far_keys, bank_keys], axis=0)
    value_set = jnp.concatenate([own_values, far_values, bank_values], axis=0)
    query_heads = query.reshape(row_count, head_count, HD)
    key_heads = key_set.reshape(-1, head_count, HD)
    value_heads = value_set.reshape(-1, head_count, HD)
    scores = jnp.einsum(
        "qhd,khd->hqk", query_heads, key_heads, preferred_element_type=jnp.float32
    ) * HD ** (-0.5)
    row_peak = jnp.max(scores, axis=2, keepdims=True)
    exponent = jnp.exp(scores - row_peak)
    denominator = jnp.sum(exponent, axis=2)
    weights = exponent.astype(jnp.bfloat16)
    combined = jnp.einsum("hqk,khd->qhd", weights, value_heads, preferred_element_type=jnp.float32)
    return (combined / denominator.T[:, :, None]).reshape(row_count, width).astype(jnp.bfloat16)


def shards(
    queries,
    keys,
    values,
    q_gain,
    k_gain,
    ref_keys,
    ref_values,
    out_weight,
    partners,
    owners,
    labels,
):
    tokens, width = queries.shape
    blocks = tokens // BLK
    n_ctx = partners.shape[0]
    persons = partners.shape[1]
    bank_rows = ref_keys.shape[0]
    piece = bank_rows // n_ctx
    own_index = lax.axis_index("ctx")
    q_float = queries.astype(jnp.float32)
    k_float = keys.astype(jnp.float32)
    n_head = lax.axis_size("head")
    squares = jnp.stack([jnp.sum(q_float * q_float, axis=1), jnp.sum(k_float * k_float, axis=1)])
    q_total, k_total = jnp.sum(gather_all(squares, "head", "ctx", n_head, 1), axis=0)
    q_norm = normalize(q_float, q_gain, q_total)
    k_factor = lax.rsqrt(k_total / D + epsilon)
    k_norm = (k_float * k_factor[:, None] * k_gain[None, :]).astype(jnp.bfloat16)
    query_blocks = q_norm.reshape(blocks, BLK, width)
    key_blocks = keys.reshape(blocks, BLK, width)
    value_blocks = values.reshape(blocks, BLK, width)

    flat = partners.reshape(n_ctx, -1)
    hit = (flat // blocks) == own_index
    pick = jnp.sum(jnp.where(hit, flat % blocks, 0), axis=1)
    kv_blocks = jnp.stack([key_blocks, value_blocks], axis=1)
    send = kv_blocks[pick]
    got = lax.all_to_all(send, "ctx", 0, 0, tiled=True)
    got_bank = scatter_bank(ref_keys, ref_values, "ctx", "head", n_ctx, 3)

    sources = (partners[own_index] // blocks).reshape(-1)
    factor_all = gather_all(k_factor.reshape(blocks, BLK), "ctx", "head", n_ctx, 4)
    far_factor = factor_all[partners[own_index] // blocks, partners[own_index] % blocks]
    far_factor = far_factor.reshape(persons, -1, 1)
    mine = got_bank[owners]
    whole = gather_all(mine.reshape(-1, width), "ctx", "head", n_ctx, 2)
    attended = attend(
        labels, sources, q_norm, k_norm, values, far_factor, k_gain, got, whole, n_ctx, partners.shape[2]
    )
    partial_out = jnp.dot(attended, out_weight, preferred_element_type=jnp.float32)
    mixed = lax.psum_scatter(
        partial_out.astype(jnp.bfloat16), "head", scatter_dimension=1, tiled=True
    )
    return (attended, mixed)


def solution(mesh):
    return jax.shard_map(
        shards,
        mesh=mesh,
        in_specs=(
            P("ctx", "head"),
            P("ctx", "head"),
            P("ctx", "head"),
            P("head"),
            P("head"),
            P("ctx", "head"),
            P("ctx", "head"),
            P("head", None),
            P(),
            P(),
            P("ctx"),
        ),
        out_specs=(P("ctx", "head"), P("ctx", "head")),
        check_vma=False,
    )
```

```python
import functools

import jax
import jax.numpy as jnp
from jax import lax
from jax.experimental import pallas as pl
from jax.experimental.pallas import tpu as pltpu
from jax.sharding import PartitionSpec as P

MESH = pl.DeviceIdType.MESH

D = 5120
HD = 128
BLK = 128


epsilon = 1e-06


def gather_kernel(axis, other_axis, n, piece_ref, out_ref, send_sem, recv_sem, local_sem):
    me = lax.axis_index(axis)
    other = lax.axis_index(other_axis)

    def device(j):
        return (j, other) if axis == "ctx" else (other, j)

    barrier = pltpu.get_barrier_semaphore()
    for k in range(1, n):
        pl.semaphore_signal(barrier, inc=1, device_id=device(lax.rem(me + k, n)), device_id_type=MESH)
    pl.semaphore_wait(barrier, n - 1)
    local = pltpu.make_async_copy(piece_ref, out_ref.at[me], local_sem)
    local.start()
    sends = []
    for k in range(1, n):
        copy = pltpu.make_async_remote_copy(
            src_ref=piece_ref,
            dst_ref=out_ref.at[me],
            send_sem=send_sem.at[k],
            recv_sem=recv_sem.at[k],
            device_id=device(lax.rem(me + k, n)),
            device_id_type=MESH,
        )
        copy.start()
        sends.append(copy)
    local.wait()
    for copy in sends:
        copy.wait_send()
    for k in range(1, n):
        source = lax.rem(me + n - k, n)
        pltpu.make_async_remote_copy(
            src_ref=piece_ref,
            dst_ref=out_ref.at[source],
            send_sem=send_sem.at[k],
            recv_sem=recv_sem.at[k],
            device_id=device(source),
            device_id_type=MESH,
        ).wait_recv()


def scatter_kernel(axis, other_axis, n, piece, keys_ref, values_ref, out_ref, send_sem, recv_sem, local_sem):
    me = lax.axis_index(axis)
    other = lax.axis_index(other_axis)

    def device(j):
        return (j, other) if axis == "ctx" else (other, j)

    def rows(j):
        return pl.ds(pl.multiple_of(j * piece, piece), piece)

    barrier = pltpu.get_barrier_semaphore()
    for k in range(1, n):
        pl.semaphore_signal(barrier, inc=1, device_id=device(lax.rem(me + k, n)), device_id_type=MESH)
    pl.semaphore_wait(barrier, n - 1)
    sources = (keys_ref, values_ref)
    local = [
        pltpu.make_async_copy(src.at[rows(me)], out_ref.at[me, t], local_sem.at[t])
        for t, src in enumerate(sources)
    ]
    for copy in local:
        copy.start()
    sends = []
    for k in range(1, n):
        peer = lax.rem(me + k, n)
        for t, src in enumerate(sources):
            copy = pltpu.make_async_remote_copy(
                src_ref=src.at[rows(peer)],
                dst_ref=out_ref.at[me, t],
                send_sem=send_sem.at[k, t],
                recv_sem=recv_sem.at[k, t],
                device_id=device(peer),
                device_id_type=MESH,
            )
            copy.start()
            sends.append(copy)
    for copy in local:
        copy.wait()
    for copy in sends:
        copy.wait_send()
    for k in range(1, n):
        source = lax.rem(me + n - k, n)
        for t, src in enumerate(sources):
            pltpu.make_async_remote_copy(
                src_ref=src.at[rows(me)],
                dst_ref=out_ref.at[source, t],
                send_sem=send_sem.at[k, t],
                recv_sem=recv_sem.at[k, t],
                device_id=device(source),
                device_id_type=MESH,
            ).wait_recv()


def scatter_bank(ref_keys, ref_values, axis, other_axis, n, collective_id):
    rows, width = ref_keys.shape
    piece = rows // n
    return pl.pallas_call(
        functools.partial(scatter_kernel, axis, other_axis, n, piece),
        out_shape=jax.ShapeDtypeStruct((n, 2, piece, width), ref_keys.dtype),
        in_specs=[pl.BlockSpec(memory_space=pl.ANY)] * 2,
        out_specs=pl.BlockSpec(memory_space=pl.ANY),
        scratch_shapes=[
            pltpu.SemaphoreType.DMA((n, 2)),
            pltpu.SemaphoreType.DMA((n, 2)),
            pltpu.SemaphoreType.DMA((2,)),
        ],
        compiler_params=pltpu.CompilerParams(collective_id=collective_id, has_side_effects=True),
    )(ref_keys, ref_values)


def gather_all(piece, axis, other_axis, n, collective_id):
    return pl.pallas_call(
        functools.partial(gather_kernel, axis, other_axis, n),
        out_shape=jax.ShapeDtypeStruct((n,) + piece.shape, piece.dtype),
        in_specs=[pl.BlockSpec(memory_space=pl.ANY)],
        out_specs=pl.BlockSpec(memory_space=pl.ANY),
        scratch_shapes=[
            pltpu.SemaphoreType.DMA((n,)),
            pltpu.SemaphoreType.DMA((n,)),
            pltpu.SemaphoreType.DMA(()),
        ],
        compiler_params=pltpu.CompilerParams(collective_id=collective_id, has_side_effects=True),
    )(piece)


def attend_kernel(
    label_ref, source_ref, q_ref, k_ref, v_ref, got_ref, whole_ref, o_ref,
    far_k, far_v, bank_k, bank_v, sem_k, sem_v, sem_bank,
):
    position = pl.program_id(0)
    person = label_ref[position]
    far_count = far_k.shape[0] // BLK
    piece = bank_k.shape[1]
    copies = []
    for j in range(far_count):
        source = source_ref[person * far_count + j]
        copies.append(pltpu.make_async_copy(
            got_ref.at[source, 0, pl.ds(0, BLK)], far_k.at[pl.ds(j * BLK, BLK)], sem_k.at[j]))
        copies.append(pltpu.make_async_copy(
            got_ref.at[source, 1, pl.ds(0, BLK)], far_v.at[pl.ds(j * BLK, BLK)], sem_v.at[j]))
    copies.append(pltpu.make_async_copy(
        whole_ref.at[:, pl.ds(person * 2 * piece, piece)], bank_k, sem_bank.at[0]))
    copies.append(pltpu.make_async_copy(
        whole_ref.at[:, pl.ds(person * 2 * piece + piece, piece)], bank_v, sem_bank.at[1]))
    for copy in copies:
        copy.start()
    for copy in copies:
        copy.wait()
    rows, width = q_ref.shape
    bank_rows = bank_k.shape[0] * piece
    dims = (((1,), (1,)), ((), ()))
    for h in range(width // HD):
        cols = pl.ds(h * HD, HD)
        query = q_ref[:, cols]
        parts = [
            (k_ref[:, cols], v_ref[:, cols]),
            (far_k[:, cols], far_v[:, cols]),
            (bank_k[:, :, cols].reshape(bank_rows, HD), bank_v[:, :, cols].reshape(bank_rows, HD)),
        ]
        scores = [
            lax.dot_general(query, key, dims, preferred_element_type=jnp.float32) * HD ** (-0.5)
            for key, _ in parts
        ]
        peak = jnp.max(scores[0], axis=1, keepdims=True)
        for score in scores[1:]:
            peak = jnp.maximum(peak, jnp.max(score, axis=1, keepdims=True))
        total = None
        summed = None
        for score, (_, value) in zip(scores, parts):
            exponent = jnp.exp(score - peak)
            part_sum = jnp.sum(exponent, axis=1, keepdims=True)
            product = jnp.dot(exponent.astype(jnp.bfloat16), value, preferred_element_type=jnp.float32)
            total = part_sum if total is None else total + part_sum
            summed = product if summed is None else summed + product
        o_ref[:, cols] = (summed / total).astype(o_ref.dtype)


def attend(labels, sources, q_norm, k_norm, values, got, whole, n_ctx, far_count):
    rows, width = q_norm.shape
    piece = whole.shape[1] // 4
    block = pl.BlockSpec((BLK, width), lambda b, lab, src: (b, 0))
    return pl.pallas_call(
        attend_kernel,
        out_shape=jax.ShapeDtypeStruct((rows, width), jnp.bfloat16),
        grid_spec=pltpu.PrefetchScalarGridSpec(
            num_scalar_prefetch=2,
            grid=(rows // BLK,),
            in_specs=[block, block, block, pl.BlockSpec(memory_space=pl.ANY), pl.BlockSpec(memory_space=pl.ANY)],
            out_specs=block,
            scratch_shapes=[
                pltpu.VMEM((far_count * BLK, width), jnp.bfloat16),
                pltpu.VMEM((far_count * BLK, width), jnp.bfloat16),
                pltpu.VMEM((n_ctx, piece, width), jnp.bfloat16),
                pltpu.VMEM((n_ctx, piece, width), jnp.bfloat16),
                pltpu.SemaphoreType.DMA((far_count,)),
                pltpu.SemaphoreType.DMA((far_count,)),
                pltpu.SemaphoreType.DMA((2,)),
            ],
        ),
        compiler_params=pltpu.CompilerParams(dimension_semantics=("arbitrary",)),
    )(labels, sources, q_norm, k_norm, values, got, whole)


def normalize(features, scale_gain, square_total):
    factor = lax.rsqrt(square_total / D + epsilon)
    return (features * factor[:, None] * scale_gain[None, :]).astype(jnp.bfloat16)


def attend_block(query, own_keys, own_values, far_keys, far_values, bank_keys, bank_values):
    row_count, width = query.shape
    head_count = width // HD
    key_set = jnp.concatenate([own_keys, far_keys, bank_keys], axis=0)
    value_set = jnp.concatenate([own_values, far_values, bank_values], axis=0)
    query_heads = query.reshape(row_count, head_count, HD)
    key_heads = key_set.reshape(-1, head_count, HD)
    value_heads = value_set.reshape(-1, head_count, HD)
    scores = jnp.einsum(
        "qhd,khd->hqk", query_heads, key_heads, preferred_element_type=jnp.float32
    ) * HD ** (-0.5)
    row_peak = jnp.max(scores, axis=2, keepdims=True)
    exponent = jnp.exp(scores - row_peak)
    denominator = jnp.sum(exponent, axis=2)
    weights = exponent.astype(jnp.bfloat16)
    combined = jnp.einsum("hqk,khd->qhd", weights, value_heads, preferred_element_type=jnp.float32)
    return (combined / denominator.T[:, :, None]).reshape(row_count, width).astype(jnp.bfloat16)


def shards(
    queries,
    keys,
    values,
    q_gain,
    k_gain,
    ref_keys,
    ref_values,
    out_weight,
    partners,
    owners,
    labels,
):
    tokens, width = queries.shape
    blocks = tokens // BLK
    n_ctx = partners.shape[0]
    persons = partners.shape[1]
    bank_rows = ref_keys.shape[0]
    piece = bank_rows // n_ctx
    own_index = lax.axis_index("ctx")
    q_float = queries.astype(jnp.float32)
    k_float = keys.astype(jnp.float32)
    n_head = lax.axis_size("head")
    squares = jnp.stack([jnp.sum(q_float * q_float, axis=1), jnp.sum(k_float * k_float, axis=1)])
    q_total, k_total = jnp.sum(gather_all(squares, "head", "ctx", n_head, 1), axis=0)
    q_norm = normalize(q_float, q_gain, q_total)
    k_norm = normalize(k_float, k_gain, k_total)
    query_blocks = q_norm.reshape(blocks, BLK, width)
    key_blocks = k_norm.reshape(blocks, BLK, width)
    value_blocks = values.reshape(blocks, BLK, width)

    flat = partners.reshape(n_ctx, -1)
    hit = (flat // blocks) == own_index
    pick = jnp.sum(jnp.where(hit, flat % blocks, 0), axis=1)
    kv_blocks = jnp.stack([key_blocks, value_blocks], axis=1)
    send = kv_blocks[pick]
    got = lax.all_to_all(send, "ctx", 0, 0, tiled=True)
    got_bank = scatter_bank(ref_keys, ref_values, "ctx", "head", n_ctx, 3)

    sources = (partners[own_index] // blocks).reshape(-1)
    mine = got_bank[owners]
    piece_rows = mine.reshape(-1, width)
    whole = lax.all_to_all(
        jnp.broadcast_to(piece_rows, (n_ctx,) + piece_rows.shape), "ctx", 0, 0, tiled=True
    )
    attended = attend(labels, sources, q_norm, k_norm, values, got, whole, n_ctx, partners.shape[2])
    partial_out = jnp.dot(attended, out_weight, preferred_element_type=jnp.float32)
    mixed = lax.psum_scatter(
        partial_out.astype(jnp.bfloat16), "head", scatter_dimension=1, tiled=True
    )
    return (attended, mixed)


def solution(mesh):
    return jax.shard_map(
        shards,
        mesh=mesh,
        in_specs=(
            P("ctx", "head"),
            P("ctx", "head"),
            P("ctx", "head"),
            P("head"),
            P("head"),
            P("ctx", "head"),
            P("ctx", "head"),
            P("head", None),
            P(),
            P(),
            P("ctx"),
        ),
        out_specs=(P("ctx", "head"), P("ctx", "head")),
        check_vma=False,
    )
```

```python
import functools

import jax
import jax.numpy as jnp
from jax import lax
from jax.experimental import pallas as pl
from jax.experimental.pallas import tpu as pltpu
from jax.sharding import PartitionSpec as P

MESH = pl.DeviceIdType.MESH

D = 5120
HD = 128
BLK = 128


epsilon = 1e-06


def gather_kernel(axis, other_axis, n, piece_ref, out_ref, send_sem, recv_sem, local_sem):
    me = lax.axis_index(axis)
    other = lax.axis_index(other_axis)

    def device(j):
        return (j, other) if axis == "ctx" else (other, j)

    barrier = pltpu.get_barrier_semaphore()
    for k in range(1, n):
        pl.semaphore_signal(barrier, inc=1, device_id=device(lax.rem(me + k, n)), device_id_type=MESH)
    pl.semaphore_wait(barrier, n - 1)
    local = pltpu.make_async_copy(piece_ref, out_ref.at[me], local_sem)
    local.start()
    sends = []
    for k in range(1, n):
        copy = pltpu.make_async_remote_copy(
            src_ref=piece_ref,
            dst_ref=out_ref.at[me],
            send_sem=send_sem.at[k],
            recv_sem=recv_sem.at[k],
            device_id=device(lax.rem(me + k, n)),
            device_id_type=MESH,
        )
        copy.start()
        sends.append(copy)
    local.wait()
    for copy in sends:
        copy.wait_send()
    for k in range(1, n):
        source = lax.rem(me + n - k, n)
        pltpu.make_async_remote_copy(
            src_ref=piece_ref,
            dst_ref=out_ref.at[source],
            send_sem=send_sem.at[k],
            recv_sem=recv_sem.at[k],
            device_id=device(source),
            device_id_type=MESH,
        ).wait_recv()


def scatter_kernel(axis, other_axis, n, piece, keys_ref, values_ref, out_ref, send_sem, recv_sem, local_sem):
    me = lax.axis_index(axis)
    other = lax.axis_index(other_axis)

    def device(j):
        return (j, other) if axis == "ctx" else (other, j)

    def rows(j):
        return pl.ds(pl.multiple_of(j * piece, piece), piece)

    barrier = pltpu.get_barrier_semaphore()
    for k in range(1, n):
        pl.semaphore_signal(barrier, inc=1, device_id=device(lax.rem(me + k, n)), device_id_type=MESH)
    pl.semaphore_wait(barrier, n - 1)
    sources = (keys_ref, values_ref)
    local = [
        pltpu.make_async_copy(src.at[rows(me)], out_ref.at[me, t], local_sem.at[t])
        for t, src in enumerate(sources)
    ]
    for copy in local:
        copy.start()
    sends = []
    for k in range(1, n):
        peer = lax.rem(me + k, n)
        for t, src in enumerate(sources):
            copy = pltpu.make_async_remote_copy(
                src_ref=src.at[rows(peer)],
                dst_ref=out_ref.at[me, t],
                send_sem=send_sem.at[k, t],
                recv_sem=recv_sem.at[k, t],
                device_id=device(peer),
                device_id_type=MESH,
            )
            copy.start()
            sends.append(copy)
    for copy in local:
        copy.wait()
    for copy in sends:
        copy.wait_send()
    for k in range(1, n):
        source = lax.rem(me + n - k, n)
        for t, src in enumerate(sources):
            pltpu.make_async_remote_copy(
                src_ref=src.at[rows(me)],
                dst_ref=out_ref.at[source, t],
                send_sem=send_sem.at[k, t],
                recv_sem=recv_sem.at[k, t],
                device_id=device(source),
                device_id_type=MESH,
            ).wait_recv()


def scatter_bank(ref_keys, ref_values, axis, other_axis, n, collective_id):
    rows, width = ref_keys.shape
    piece = rows // n
    return pl.pallas_call(
        functools.partial(scatter_kernel, axis, other_axis, n, piece),
        out_shape=jax.ShapeDtypeStruct((n, 2, piece, width), ref_keys.dtype),
        in_specs=[pl.BlockSpec(memory_space=pl.ANY)] * 2,
        out_specs=pl.BlockSpec(memory_space=pl.ANY),
        scratch_shapes=[
            pltpu.SemaphoreType.DMA((n, 2)),
            pltpu.SemaphoreType.DMA((n, 2)),
            pltpu.SemaphoreType.DMA((2,)),
        ],
        compiler_params=pltpu.CompilerParams(collective_id=collective_id, has_side_effects=True),
    )(ref_keys, ref_values)


def gather_all(piece, axis, other_axis, n, collective_id):
    return pl.pallas_call(
        functools.partial(gather_kernel, axis, other_axis, n),
        out_shape=jax.ShapeDtypeStruct((n,) + piece.shape, piece.dtype),
        in_specs=[pl.BlockSpec(memory_space=pl.ANY)],
        out_specs=pl.BlockSpec(memory_space=pl.ANY),
        scratch_shapes=[
            pltpu.SemaphoreType.DMA((n,)),
            pltpu.SemaphoreType.DMA((n,)),
            pltpu.SemaphoreType.DMA(()),
        ],
        compiler_params=pltpu.CompilerParams(collective_id=collective_id, has_side_effects=True),
    )(piece)


def attend_kernel(
    label_ref, source_ref, q_ref, k_ref, v_ref, got_ref, whole_ref, o_ref,
    far_k, far_v, bank_k, bank_v, sem_k, sem_v, sem_bank,
):
    position = pl.program_id(0)
    person = label_ref[position]
    far_count = far_k.shape[0] // BLK
    piece = bank_k.shape[1]
    copies = []
    for j in range(far_count):
        source = source_ref[person * far_count + j]
        copies.append(pltpu.make_async_copy(
            got_ref.at[source, 0, pl.ds(0, BLK)], far_k.at[pl.ds(j * BLK, BLK)], sem_k.at[j]))
        copies.append(pltpu.make_async_copy(
            got_ref.at[source, 1, pl.ds(0, BLK)], far_v.at[pl.ds(j * BLK, BLK)], sem_v.at[j]))
    copies.append(pltpu.make_async_copy(
        whole_ref.at[:, pl.ds(person * 2 * piece, piece)], bank_k, sem_bank.at[0]))
    copies.append(pltpu.make_async_copy(
        whole_ref.at[:, pl.ds(person * 2 * piece + piece, piece)], bank_v, sem_bank.at[1]))
    for copy in copies:
        copy.start()
    for copy in copies:
        copy.wait()
    rows, width = q_ref.shape
    bank_rows = bank_k.shape[0] * piece
    dims = (((1,), (1,)), ((), ()))
    for h in range(width // HD):
        cols = pl.ds(h * HD, HD)
        query = q_ref[:, cols]
        parts = [
            (k_ref[:, cols], v_ref[:, cols]),
            (far_k[:, cols], far_v[:, cols]),
            (bank_k[:, :, cols].reshape(bank_rows, HD), bank_v[:, :, cols].reshape(bank_rows, HD)),
        ]
        scores = [
            lax.dot_general(query, key, dims, preferred_element_type=jnp.float32) * HD ** (-0.5)
            for key, _ in parts
        ]
        peak = jnp.max(scores[0], axis=1, keepdims=True)
        for score in scores[1:]:
            peak = jnp.maximum(peak, jnp.max(score, axis=1, keepdims=True))
        total = None
        summed = None
        for score, (_, value) in zip(scores, parts):
            exponent = jnp.exp(score - peak)
            part_sum = jnp.sum(exponent, axis=1, keepdims=True)
            product = jnp.dot(exponent.astype(jnp.bfloat16), value, preferred_element_type=jnp.float32)
            total = part_sum if total is None else total + part_sum
            summed = product if summed is None else summed + product
        o_ref[:, cols] = (summed / total).astype(o_ref.dtype)


def attend(labels, sources, q_norm, k_norm, values, got, whole, n_ctx, far_count):
    rows, width = q_norm.shape
    piece = whole.shape[1] // 4
    block = pl.BlockSpec((BLK, width), lambda b, lab, src: (b, 0))
    return pl.pallas_call(
        attend_kernel,
        out_shape=jax.ShapeDtypeStruct((rows, width), jnp.bfloat16),
        grid_spec=pltpu.PrefetchScalarGridSpec(
            num_scalar_prefetch=2,
            grid=(rows // BLK,),
            in_specs=[block, block, block, pl.BlockSpec(memory_space=pl.ANY), pl.BlockSpec(memory_space=pl.ANY)],
            out_specs=block,
            scratch_shapes=[
                pltpu.VMEM((far_count * BLK, width), jnp.bfloat16),
                pltpu.VMEM((far_count * BLK, width), jnp.bfloat16),
                pltpu.VMEM((n_ctx, piece, width), jnp.bfloat16),
                pltpu.VMEM((n_ctx, piece, width), jnp.bfloat16),
                pltpu.SemaphoreType.DMA((far_count,)),
                pltpu.SemaphoreType.DMA((far_count,)),
                pltpu.SemaphoreType.DMA((2,)),
            ],
        ),
        compiler_params=pltpu.CompilerParams(dimension_semantics=("arbitrary",)),
    )(labels, sources, q_norm, k_norm, values, got, whole)


def normalize(features, scale_gain, square_total):
    factor = lax.rsqrt(square_total / D + epsilon)
    return (features * factor[:, None] * scale_gain[None, :]).astype(jnp.bfloat16)


def attend_block(query, own_keys, own_values, far_keys, far_values, bank_keys, bank_values):
    row_count, width = query.shape
    head_count = width // HD
    key_set = jnp.concatenate([own_keys, far_keys, bank_keys], axis=0)
    value_set = jnp.concatenate([own_values, far_values, bank_values], axis=0)
    query_heads = query.reshape(row_count, head_count, HD)
    key_heads = key_set.reshape(-1, head_count, HD)
    value_heads = value_set.reshape(-1, head_count, HD)
    scores = jnp.einsum(
        "qhd,khd->hqk", query_heads, key_heads, preferred_element_type=jnp.float32
    ) * HD ** (-0.5)
    row_peak = jnp.max(scores, axis=2, keepdims=True)
    exponent = jnp.exp(scores - row_peak)
    denominator = jnp.sum(exponent, axis=2)
    weights = exponent.astype(jnp.bfloat16)
    combined = jnp.einsum("hqk,khd->qhd", weights, value_heads, preferred_element_type=jnp.float32)
    return (combined / denominator.T[:, :, None]).reshape(row_count, width).astype(jnp.bfloat16)


def shards(
    queries,
    keys,
    values,
    q_gain,
    k_gain,
    ref_keys,
    ref_values,
    out_weight,
    partners,
    owners,
    labels,
):
    tokens, width = queries.shape
    blocks = tokens // BLK
    n_ctx = partners.shape[0]
    persons = partners.shape[1]
    bank_rows = ref_keys.shape[0]
    piece = bank_rows // n_ctx
    own_index = lax.axis_index("ctx")
    q_float = queries.astype(jnp.float32)
    k_float = keys.astype(jnp.float32)
    n_head = lax.axis_size("head")
    squares = jnp.stack([jnp.sum(q_float * q_float, axis=1), jnp.sum(k_float * k_float, axis=1)])
    q_total, k_total = jnp.sum(gather_all(squares, "head", "ctx", n_head, 1), axis=0)
    q_norm = normalize(q_float, q_gain, q_total)
    k_norm = normalize(k_float, k_gain, k_total)
    query_blocks = q_norm.reshape(blocks, BLK, width)
    key_blocks = k_norm.reshape(blocks, BLK, width)
    value_blocks = values.reshape(blocks, BLK, width)

    flat = partners.reshape(n_ctx, -1)
    hit = (flat // blocks) == own_index
    pick = jnp.sum(jnp.where(hit, flat % blocks, 0), axis=1)
    kv_blocks = jnp.stack([key_blocks, value_blocks], axis=1)
    send_blocks = kv_blocks[pick]
    bank = jnp.stack([ref_keys, ref_values]).reshape(2, n_ctx, piece, width)
    send_bank = jnp.transpose(bank, (1, 0, 2, 3))
    send = jnp.concatenate([send_blocks, send_bank], axis=2)
    got = lax.all_to_all(send, "ctx", 0, 0, tiled=True)
    got_bank = got[:, :, BLK:]

    sources = (partners[own_index] // blocks).reshape(-1)
    mine = got_bank[owners]
    piece_rows = mine.reshape(-1, width)
    whole = lax.all_to_all(
        jnp.broadcast_to(piece_rows, (n_ctx,) + piece_rows.shape), "ctx", 0, 0, tiled=True
    )
    attended = attend(labels, sources, q_norm, k_norm, values, got, whole, n_ctx, partners.shape[2])
    partial_out = jnp.dot(attended, out_weight, preferred_element_type=jnp.float32)
    mixed = lax.psum_scatter(
        partial_out.astype(jnp.bfloat16), "head", scatter_dimension=1, tiled=True
    )
    return (attended, mixed)


def solution(mesh):
    return jax.shard_map(
        shards,
        mesh=mesh,
        in_specs=(
            P("ctx", "head"),
            P("ctx", "head"),
            P("ctx", "head"),
            P("head"),
            P("head"),
            P("ctx", "head"),
            P("ctx", "head"),
            P("head", None),
            P(),
            P(),
            P("ctx"),
        ),
        out_specs=(P("ctx", "head"), P("ctx", "head")),
        check_vma=False,
    )
```

```python
import functools

import jax
import jax.numpy as jnp
from jax import lax
from jax.experimental import pallas as pl
from jax.experimental.pallas import tpu as pltpu
from jax.sharding import PartitionSpec as P

MESH = pl.DeviceIdType.MESH

D = 5120
HD = 128
BLK = 128


epsilon = 1e-06


def gather_kernel(axis, other_axis, n, piece_ref, out_ref, send_sem, recv_sem, local_sem):
    me = lax.axis_index(axis)
    other = lax.axis_index(other_axis)

    def device(j):
        return (j, other) if axis == "ctx" else (other, j)

    barrier = pltpu.get_barrier_semaphore()
    for k in range(1, n):
        pl.semaphore_signal(barrier, inc=1, device_id=device(lax.rem(me + k, n)), device_id_type=MESH)
    pl.semaphore_wait(barrier, n - 1)
    local = pltpu.make_async_copy(piece_ref, out_ref.at[me], local_sem)
    local.start()
    sends = []
    for k in range(1, n):
        copy = pltpu.make_async_remote_copy(
            src_ref=piece_ref,
            dst_ref=out_ref.at[me],
            send_sem=send_sem.at[k],
            recv_sem=recv_sem.at[k],
            device_id=device(lax.rem(me + k, n)),
            device_id_type=MESH,
        )
        copy.start()
        sends.append(copy)
    local.wait()
    for copy in sends:
        copy.wait_send()
    for k in range(1, n):
        source = lax.rem(me + n - k, n)
        pltpu.make_async_remote_copy(
            src_ref=piece_ref,
            dst_ref=out_ref.at[source],
            send_sem=send_sem.at[k],
            recv_sem=recv_sem.at[k],
            device_id=device(source),
            device_id_type=MESH,
        ).wait_recv()


def scatter_kernel(axis, other_axis, n, piece, keys_ref, values_ref, out_ref, send_sem, recv_sem, local_sem):
    me = lax.axis_index(axis)
    other = lax.axis_index(other_axis)

    def device(j):
        return (j, other) if axis == "ctx" else (other, j)

    def rows(j):
        return pl.ds(pl.multiple_of(j * piece, piece), piece)

    barrier = pltpu.get_barrier_semaphore()
    for k in range(1, n):
        pl.semaphore_signal(barrier, inc=1, device_id=device(lax.rem(me + k, n)), device_id_type=MESH)
    pl.semaphore_wait(barrier, n - 1)
    sources = (keys_ref, values_ref)
    local = [
        pltpu.make_async_copy(src.at[rows(me)], out_ref.at[me, t], local_sem.at[t])
        for t, src in enumerate(sources)
    ]
    for copy in local:
        copy.start()
    sends = []
    for k in range(1, n):
        peer = lax.rem(me + k, n)
        for t, src in enumerate(sources):
            copy = pltpu.make_async_remote_copy(
                src_ref=src.at[rows(peer)],
                dst_ref=out_ref.at[me, t],
                send_sem=send_sem.at[k, t],
                recv_sem=recv_sem.at[k, t],
                device_id=device(peer),
                device_id_type=MESH,
            )
            copy.start()
            sends.append(copy)
    for copy in local:
        copy.wait()
    for copy in sends:
        copy.wait_send()
    for k in range(1, n):
        source = lax.rem(me + n - k, n)
        for t, src in enumerate(sources):
            pltpu.make_async_remote_copy(
                src_ref=src.at[rows(me)],
                dst_ref=out_ref.at[source, t],
                send_sem=send_sem.at[k, t],
                recv_sem=recv_sem.at[k, t],
                device_id=device(source),
                device_id_type=MESH,
            ).wait_recv()


def scatter_bank(ref_keys, ref_values, axis, other_axis, n, collective_id):
    rows, width = ref_keys.shape
    piece = rows // n
    return pl.pallas_call(
        functools.partial(scatter_kernel, axis, other_axis, n, piece),
        out_shape=jax.ShapeDtypeStruct((n, 2, piece, width), ref_keys.dtype),
        in_specs=[pl.BlockSpec(memory_space=pl.ANY)] * 2,
        out_specs=pl.BlockSpec(memory_space=pl.ANY),
        scratch_shapes=[
            pltpu.SemaphoreType.DMA((n, 2)),
            pltpu.SemaphoreType.DMA((n, 2)),
            pltpu.SemaphoreType.DMA((2,)),
        ],
        compiler_params=pltpu.CompilerParams(collective_id=collective_id, has_side_effects=True),
    )(ref_keys, ref_values)


def gather_all(piece, axis, other_axis, n, collective_id):
    return pl.pallas_call(
        functools.partial(gather_kernel, axis, other_axis, n),
        out_shape=jax.ShapeDtypeStruct((n,) + piece.shape, piece.dtype),
        in_specs=[pl.BlockSpec(memory_space=pl.ANY)],
        out_specs=pl.BlockSpec(memory_space=pl.ANY),
        scratch_shapes=[
            pltpu.SemaphoreType.DMA((n,)),
            pltpu.SemaphoreType.DMA((n,)),
            pltpu.SemaphoreType.DMA(()),
        ],
        compiler_params=pltpu.CompilerParams(collective_id=collective_id, has_side_effects=True),
    )(piece)


def attend_kernel(
    label_ref, source_ref, q_ref, k_ref, v_ref, got_ref, whole_ref, o_ref,
    far_k, far_v, bank_k, bank_v, sem_k, sem_v, sem_bank,
):
    position = pl.program_id(0)
    person = label_ref[position]
    far_count = far_k.shape[0] // BLK
    piece = bank_k.shape[1]
    copies = []
    for j in range(far_count):
        source = source_ref[person * far_count + j]
        copies.append(pltpu.make_async_copy(
            got_ref.at[source, 0, pl.ds(0, BLK)], far_k.at[pl.ds(j * BLK, BLK)], sem_k.at[j]))
        copies.append(pltpu.make_async_copy(
            got_ref.at[source, 1, pl.ds(0, BLK)], far_v.at[pl.ds(j * BLK, BLK)], sem_v.at[j]))
    copies.append(pltpu.make_async_copy(
        whole_ref.at[:, pl.ds(person * 2 * piece, piece)], bank_k, sem_bank.at[0]))
    copies.append(pltpu.make_async_copy(
        whole_ref.at[:, pl.ds(person * 2 * piece + piece, piece)], bank_v, sem_bank.at[1]))
    for copy in copies:
        copy.start()
    for copy in copies:
        copy.wait()
    rows, width = q_ref.shape
    bank_rows = bank_k.shape[0] * piece
    dims = (((1,), (1,)), ((), ()))
    for h in range(width // HD):
        cols = pl.ds(h * HD, HD)
        query = q_ref[:, cols]
        parts = [
            (k_ref[:, cols], v_ref[:, cols]),
            (far_k[:, cols], far_v[:, cols]),
            (bank_k[:, :, cols].reshape(bank_rows, HD), bank_v[:, :, cols].reshape(bank_rows, HD)),
        ]
        scores = [
            lax.dot_general(query, key, dims, preferred_element_type=jnp.float32) * HD ** (-0.5)
            for key, _ in parts
        ]
        peak = jnp.max(scores[0], axis=1, keepdims=True)
        for score in scores[1:]:
            peak = jnp.maximum(peak, jnp.max(score, axis=1, keepdims=True))
        total = None
        summed = None
        for score, (_, value) in zip(scores, parts):
            exponent = jnp.exp(score - peak)
            part_sum = jnp.sum(exponent, axis=1, keepdims=True)
            product = jnp.dot(exponent.astype(jnp.bfloat16), value, preferred_element_type=jnp.float32)
            total = part_sum if total is None else total + part_sum
            summed = product if summed is None else summed + product
        o_ref[:, cols] = (summed / total).astype(o_ref.dtype)


def attend(labels, sources, q_norm, k_norm, values, got, whole, n_ctx, far_count):
    rows, width = q_norm.shape
    piece = whole.shape[1] // 4
    block = pl.BlockSpec((BLK, width), lambda b, lab, src: (b, 0))
    return pl.pallas_call(
        attend_kernel,
        out_shape=jax.ShapeDtypeStruct((rows, width), jnp.bfloat16),
        grid_spec=pltpu.PrefetchScalarGridSpec(
            num_scalar_prefetch=2,
            grid=(rows // BLK,),
            in_specs=[block, block, block, pl.BlockSpec(memory_space=pl.ANY), pl.BlockSpec(memory_space=pl.ANY)],
            out_specs=block,
            scratch_shapes=[
                pltpu.VMEM((far_count * BLK, width), jnp.bfloat16),
                pltpu.VMEM((far_count * BLK, width), jnp.bfloat16),
                pltpu.VMEM((n_ctx, piece, width), jnp.bfloat16),
                pltpu.VMEM((n_ctx, piece, width), jnp.bfloat16),
                pltpu.SemaphoreType.DMA((far_count,)),
                pltpu.SemaphoreType.DMA((far_count,)),
                pltpu.SemaphoreType.DMA((2,)),
            ],
        ),
        compiler_params=pltpu.CompilerParams(dimension_semantics=("arbitrary",)),
    )(labels, sources, q_norm, k_norm, values, got, whole)


def normalize(features, scale_gain, square_total):
    factor = lax.rsqrt(square_total / D + epsilon)
    return (features * factor[:, None] * scale_gain[None, :]).astype(jnp.bfloat16)


def attend_block(query, own_keys, own_values, far_keys, far_values, bank_keys, bank_values):
    row_count, width = query.shape
    head_count = width // HD
    key_set = jnp.concatenate([own_keys, far_keys, bank_keys], axis=0)
    value_set = jnp.concatenate([own_values, far_values, bank_values], axis=0)
    query_heads = query.reshape(row_count, head_count, HD)
    key_heads = key_set.reshape(-1, head_count, HD)
    value_heads = value_set.reshape(-1, head_count, HD)
    scores = jnp.einsum(
        "qhd,khd->hqk", query_heads, key_heads, preferred_element_type=jnp.float32
    ) * HD ** (-0.5)
    row_peak = jnp.max(scores, axis=2, keepdims=True)
    exponent = jnp.exp(scores - row_peak)
    denominator = jnp.sum(exponent, axis=2)
    weights = exponent.astype(jnp.bfloat16)
    combined = jnp.einsum("hqk,khd->qhd", weights, value_heads, preferred_element_type=jnp.float32)
    return (combined / denominator.T[:, :, None]).reshape(row_count, width).astype(jnp.bfloat16)


def shards(
    queries,
    keys,
    values,
    q_gain,
    k_gain,
    ref_keys,
    ref_values,
    out_weight,
    partners,
    owners,
    labels,
):
    tokens, width = queries.shape
    blocks = tokens // BLK
    n_ctx = partners.shape[0]
    persons = partners.shape[1]
    bank_rows = ref_keys.shape[0]
    piece = bank_rows // n_ctx
    own_index = lax.axis_index("ctx")
    q_float = queries.astype(jnp.float32)
    k_float = keys.astype(jnp.float32)
    n_head = lax.axis_size("head")
    squares = jnp.stack([jnp.sum(q_float * q_float, axis=1), jnp.sum(k_float * k_float, axis=1)])
    q_total, k_total = jnp.sum(gather_all(squares, "head", "ctx", n_head, 1), axis=0)
    q_norm = normalize(q_float, q_gain, q_total)
    k_norm = normalize(k_float, k_gain, k_total)
    query_blocks = q_norm.reshape(blocks, BLK, width)
    key_blocks = k_norm.reshape(blocks, BLK, width)
    value_blocks = values.reshape(blocks, BLK, width)

    flat = partners.reshape(n_ctx, -1)
    hit = (flat // blocks) == own_index
    pick = jnp.sum(jnp.where(hit, flat % blocks, 0), axis=1)
    kv_blocks = jnp.stack([key_blocks, value_blocks], axis=1)
    send = kv_blocks[pick]
    got = lax.all_to_all(send, "ctx", 0, 0, tiled=True)
    bank = jnp.stack([ref_keys, ref_values]).reshape(2, n_ctx, piece, width)
    got_bank = lax.all_to_all(jnp.transpose(bank, (1, 0, 2, 3)), "ctx", 0, 0, tiled=True)

    sources = (partners[own_index] // blocks).reshape(-1)
    mine = got_bank[owners]
    piece_rows = mine.reshape(-1, width)
    whole = lax.all_to_all(
        jnp.broadcast_to(piece_rows, (n_ctx,) + piece_rows.shape), "ctx", 0, 0, tiled=True
    )
    attended = attend(labels, sources, q_norm, k_norm, values, got, whole, n_ctx, partners.shape[2])
    partial_out = jnp.dot(attended, out_weight, preferred_element_type=jnp.float32)
    mixed = lax.psum_scatter(
        partial_out.astype(jnp.bfloat16), "head", scatter_dimension=1, tiled=True
    )
    return (attended, mixed)


def solution(mesh):
    return jax.shard_map(
        shards,
        mesh=mesh,
        in_specs=(
            P("ctx", "head"),
            P("ctx", "head"),
            P("ctx", "head"),
            P("head"),
            P("head"),
            P("ctx", "head"),
            P("ctx", "head"),
            P("head", None),
            P(),
            P(),
            P("ctx"),
        ),
        out_specs=(P("ctx", "head"), P("ctx", "head")),
        check_vma=False,
    )
```

```python
import functools

import jax
import jax.numpy as jnp
from jax import lax
from jax.experimental import pallas as pl
from jax.experimental.pallas import tpu as pltpu
from jax.sharding import PartitionSpec as P

MESH = pl.DeviceIdType.MESH

D = 5120
HD = 128
BLK = 128


epsilon = 1e-06


def gather_kernel(axis, other_axis, n, piece_ref, out_ref, send_sem, recv_sem, local_sem):
    me = lax.axis_index(axis)
    other = lax.axis_index(other_axis)

    def device(j):
        return (j, other) if axis == "ctx" else (other, j)

    barrier = pltpu.get_barrier_semaphore()
    for k in range(1, n):
        pl.semaphore_signal(barrier, inc=1, device_id=device(lax.rem(me + k, n)), device_id_type=MESH)
    pl.semaphore_wait(barrier, n - 1)
    local = pltpu.make_async_copy(piece_ref, out_ref.at[me], local_sem)
    local.start()
    sends = []
    for k in range(1, n):
        copy = pltpu.make_async_remote_copy(
            src_ref=piece_ref,
            dst_ref=out_ref.at[me],
            send_sem=send_sem.at[k],
            recv_sem=recv_sem.at[k],
            device_id=device(lax.rem(me + k, n)),
            device_id_type=MESH,
        )
        copy.start()
        sends.append(copy)
    local.wait()
    for copy in sends:
        copy.wait_send()
    for k in range(1, n):
        source = lax.rem(me + n - k, n)
        pltpu.make_async_remote_copy(
            src_ref=piece_ref,
            dst_ref=out_ref.at[source],
            send_sem=send_sem.at[k],
            recv_sem=recv_sem.at[k],
            device_id=device(source),
            device_id_type=MESH,
        ).wait_recv()


def scatter_kernel(axis, other_axis, n, piece, keys_ref, values_ref, out_ref, send_sem, recv_sem, local_sem):
    me = lax.axis_index(axis)
    other = lax.axis_index(other_axis)

    def device(j):
        return (j, other) if axis == "ctx" else (other, j)

    def rows(j):
        return pl.ds(pl.multiple_of(j * piece, piece), piece)

    barrier = pltpu.get_barrier_semaphore()
    for k in range(1, n):
        pl.semaphore_signal(barrier, inc=1, device_id=device(lax.rem(me + k, n)), device_id_type=MESH)
    pl.semaphore_wait(barrier, n - 1)
    sources = (keys_ref, values_ref)
    local = [
        pltpu.make_async_copy(src.at[rows(me)], out_ref.at[me, t], local_sem.at[t])
        for t, src in enumerate(sources)
    ]
    for copy in local:
        copy.start()
    sends = []
    for k in range(1, n):
        peer = lax.rem(me + k, n)
        for t, src in enumerate(sources):
            copy = pltpu.make_async_remote_copy(
                src_ref=src.at[rows(peer)],
                dst_ref=out_ref.at[me, t],
                send_sem=send_sem.at[k, t],
                recv_sem=recv_sem.at[k, t],
                device_id=device(peer),
                device_id_type=MESH,
            )
            copy.start()
            sends.append(copy)
    for copy in local:
        copy.wait()
    for copy in sends:
        copy.wait_send()
    for k in range(1, n):
        source = lax.rem(me + n - k, n)
        for t, src in enumerate(sources):
            pltpu.make_async_remote_copy(
                src_ref=src.at[rows(me)],
                dst_ref=out_ref.at[source, t],
                send_sem=send_sem.at[k, t],
                recv_sem=recv_sem.at[k, t],
                device_id=device(source),
                device_id_type=MESH,
            ).wait_recv()


def scatter_bank(ref_keys, ref_values, axis, other_axis, n, collective_id):
    rows, width = ref_keys.shape
    piece = rows // n
    return pl.pallas_call(
        functools.partial(scatter_kernel, axis, other_axis, n, piece),
        out_shape=jax.ShapeDtypeStruct((n, 2, piece, width), ref_keys.dtype),
        in_specs=[pl.BlockSpec(memory_space=pl.ANY)] * 2,
        out_specs=pl.BlockSpec(memory_space=pl.ANY),
        scratch_shapes=[
            pltpu.SemaphoreType.DMA((n, 2)),
            pltpu.SemaphoreType.DMA((n, 2)),
            pltpu.SemaphoreType.DMA((2,)),
        ],
        compiler_params=pltpu.CompilerParams(collective_id=collective_id, has_side_effects=True),
    )(ref_keys, ref_values)


def gather_all(piece, axis, other_axis, n, collective_id):
    return pl.pallas_call(
        functools.partial(gather_kernel, axis, other_axis, n),
        out_shape=jax.ShapeDtypeStruct((n,) + piece.shape, piece.dtype),
        in_specs=[pl.BlockSpec(memory_space=pl.ANY)],
        out_specs=pl.BlockSpec(memory_space=pl.ANY),
        scratch_shapes=[
            pltpu.SemaphoreType.DMA((n,)),
            pltpu.SemaphoreType.DMA((n,)),
            pltpu.SemaphoreType.DMA(()),
        ],
        compiler_params=pltpu.CompilerParams(collective_id=collective_id, has_side_effects=True),
    )(piece)


def attend_kernel(
    label_ref, source_ref, q_ref, k_ref, v_ref, got_ref, whole_ref, o_ref,
    far_k, far_v, bank_k, bank_v, sem_k, sem_v, sem_bank,
):
    n_blocks = far_k.shape[0]
    far_count = far_k.shape[1] // BLK
    piece = bank_k.shape[2]
    pending = []
    for position in range(n_blocks):
        person = label_ref[position]
        copies = []
        for j in range(far_count):
            source = source_ref[person * far_count + j]
            copies.append(pltpu.make_async_copy(
                got_ref.at[source, 0, pl.ds(0, BLK)], far_k.at[position, pl.ds(j * BLK, BLK)],
                sem_k.at[position, j]))
            copies.append(pltpu.make_async_copy(
                got_ref.at[source, 1, pl.ds(0, BLK)], far_v.at[position, pl.ds(j * BLK, BLK)],
                sem_v.at[position, j]))
        copies.append(pltpu.make_async_copy(
            whole_ref.at[:, pl.ds(person * 2 * piece, piece)], bank_k.at[position], sem_bank.at[position, 0]))
        copies.append(pltpu.make_async_copy(
            whole_ref.at[:, pl.ds(person * 2 * piece + piece, piece)], bank_v.at[position],
            sem_bank.at[position, 1]))
        for copy in copies:
            copy.start()
        pending.append(copies)
    width = q_ref.shape[1]
    bank_rows = bank_k.shape[1] * piece
    dims = (((1,), (1,)), ((), ()))
    for position in range(n_blocks):
        for copy in pending[position]:
            copy.wait()
        rows = pl.ds(position * BLK, BLK)
        for h in range(width // HD):
            cols = pl.ds(h * HD, HD)
            query = q_ref[rows, cols]
            parts = [
                (k_ref[rows, cols], v_ref[rows, cols]),
                (far_k[position, :, cols], far_v[position, :, cols]),
                (
                    bank_k[position, :, :, cols].reshape(bank_rows, HD),
                    bank_v[position, :, :, cols].reshape(bank_rows, HD),
                ),
            ]
            scores = [
                lax.dot_general(query, key, dims, preferred_element_type=jnp.float32) * HD ** (-0.5)
                for key, _ in parts
            ]
            peak = jnp.max(scores[0], axis=1, keepdims=True)
            for score in scores[1:]:
                peak = jnp.maximum(peak, jnp.max(score, axis=1, keepdims=True))
            total = None
            summed = None
            for score, (_, value) in zip(scores, parts):
                exponent = jnp.exp(score - peak)
                part_sum = jnp.sum(exponent, axis=1, keepdims=True)
                product = jnp.dot(exponent.astype(jnp.bfloat16), value, preferred_element_type=jnp.float32)
                total = part_sum if total is None else total + part_sum
                summed = product if summed is None else summed + product
            o_ref[rows, cols] = (summed / total).astype(o_ref.dtype)


def attend(labels, sources, q_norm, k_norm, values, got, whole, n_ctx, far_count):
    rows, width = q_norm.shape
    n_blocks = rows // BLK
    piece = whole.shape[1] // 4
    vmem = pl.BlockSpec(memory_space=pltpu.VMEM)
    smem = pl.BlockSpec(memory_space=pltpu.SMEM)
    return pl.pallas_call(
        attend_kernel,
        out_shape=jax.ShapeDtypeStruct((rows, width), jnp.bfloat16),
        in_specs=[smem, smem, vmem, vmem, vmem, pl.BlockSpec(memory_space=pl.ANY), pl.BlockSpec(memory_space=pl.ANY)],
        out_specs=vmem,
        scratch_shapes=[
            pltpu.VMEM((n_blocks, far_count * BLK, width), jnp.bfloat16),
            pltpu.VMEM((n_blocks, far_count * BLK, width), jnp.bfloat16),
            pltpu.VMEM((n_blocks, n_ctx, piece, width), jnp.bfloat16),
            pltpu.VMEM((n_blocks, n_ctx, piece, width), jnp.bfloat16),
            pltpu.SemaphoreType.DMA((n_blocks, far_count)),
            pltpu.SemaphoreType.DMA((n_blocks, far_count)),
            pltpu.SemaphoreType.DMA((n_blocks, 2)),
        ],
    )(labels, sources, q_norm, k_norm, values, got, whole)


def normalize(features, scale_gain, square_total):
    factor = lax.rsqrt(square_total / D + epsilon)
    return (features * factor[:, None] * scale_gain[None, :]).astype(jnp.bfloat16)


def attend_block(query, own_keys, own_values, far_keys, far_values, bank_keys, bank_values):
    row_count, width = query.shape
    head_count = width // HD
    key_set = jnp.concatenate([own_keys, far_keys, bank_keys], axis=0)
    value_set = jnp.concatenate([own_values, far_values, bank_values], axis=0)
    query_heads = query.reshape(row_count, head_count, HD)
    key_heads = key_set.reshape(-1, head_count, HD)
    value_heads = value_set.reshape(-1, head_count, HD)
    scores = jnp.einsum(
        "qhd,khd->hqk", query_heads, key_heads, preferred_element_type=jnp.float32
    ) * HD ** (-0.5)
    row_peak = jnp.max(scores, axis=2, keepdims=True)
    exponent = jnp.exp(scores - row_peak)
    denominator = jnp.sum(exponent, axis=2)
    weights = exponent.astype(jnp.bfloat16)
    combined = jnp.einsum("hqk,khd->qhd", weights, value_heads, preferred_element_type=jnp.float32)
    return (combined / denominator.T[:, :, None]).reshape(row_count, width).astype(jnp.bfloat16)


def shards(
    queries,
    keys,
    values,
    q_gain,
    k_gain,
    ref_keys,
    ref_values,
    out_weight,
    partners,
    owners,
    labels,
):
    tokens, width = queries.shape
    blocks = tokens // BLK
    n_ctx = partners.shape[0]
    persons = partners.shape[1]
    bank_rows = ref_keys.shape[0]
    piece = bank_rows // n_ctx
    own_index = lax.axis_index("ctx")
    q_float = queries.astype(jnp.float32)
    k_float = keys.astype(jnp.float32)
    n_head = lax.axis_size("head")
    squares = jnp.stack([jnp.sum(q_float * q_float, axis=1), jnp.sum(k_float * k_float, axis=1)])
    q_total, k_total = jnp.sum(gather_all(squares, "head", "ctx", n_head, 1), axis=0)
    q_norm = normalize(q_float, q_gain, q_total)
    k_norm = normalize(k_float, k_gain, k_total)
    query_blocks = q_norm.reshape(blocks, BLK, width)
    key_blocks = k_norm.reshape(blocks, BLK, width)
    value_blocks = values.reshape(blocks, BLK, width)

    flat = partners.reshape(n_ctx, -1)
    hit = (flat // blocks) == own_index
    pick = jnp.sum(jnp.where(hit, flat % blocks, 0), axis=1)
    kv_blocks = jnp.stack([key_blocks, value_blocks], axis=1)
    send = kv_blocks[pick]
    got = lax.all_to_all(send, "ctx", 0, 0, tiled=True)
    bank = jnp.stack([ref_keys, ref_values]).reshape(2, n_ctx, piece, width)
    got_bank = lax.all_to_all(jnp.transpose(bank, (1, 0, 2, 3)), "ctx", 0, 0, tiled=True)

    sources = (partners[own_index] // blocks).reshape(-1)
    mine = got_bank[owners]
    piece_rows = mine.reshape(-1, width)
    whole = lax.all_to_all(
        jnp.broadcast_to(piece_rows, (n_ctx,) + piece_rows.shape), "ctx", 0, 0, tiled=True
    )
    attended = attend(labels, sources, q_norm, k_norm, values, got, whole, n_ctx, partners.shape[2])
    partial_out = jnp.dot(attended, out_weight, preferred_element_type=jnp.float32)
    mixed = lax.psum_scatter(
        partial_out.astype(jnp.bfloat16), "head", scatter_dimension=1, tiled=True
    )
    return (attended, mixed)


def solution(mesh):
    return jax.shard_map(
        shards,
        mesh=mesh,
        in_specs=(
            P("ctx", "head"),
            P("ctx", "head"),
            P("ctx", "head"),
            P("head"),
            P("head"),
            P("ctx", "head"),
            P("ctx", "head"),
            P("head", None),
            P(),
            P(),
            P("ctx"),
        ),
        out_specs=(P("ctx", "head"), P("ctx", "head")),
        check_vma=False,
    )
```

```python
import functools

import jax
import jax.numpy as jnp
from jax import lax
from jax.experimental import pallas as pl
from jax.experimental.pallas import tpu as pltpu
from jax.sharding import PartitionSpec as P

MESH = pl.DeviceIdType.MESH

D = 5120
HD = 128
BLK = 128


epsilon = 1e-06


def gather_kernel(axis, other_axis, n, piece_ref, out_ref, send_sem, recv_sem, local_sem):
    me = lax.axis_index(axis)
    other = lax.axis_index(other_axis)

    def device(j):
        return (j, other) if axis == "ctx" else (other, j)

    barrier = pltpu.get_barrier_semaphore()
    for k in range(1, n):
        pl.semaphore_signal(barrier, inc=1, device_id=device(lax.rem(me + k, n)), device_id_type=MESH)
    pl.semaphore_wait(barrier, n - 1)
    local = pltpu.make_async_copy(piece_ref, out_ref.at[me], local_sem)
    local.start()
    sends = []
    for k in range(1, n):
        copy = pltpu.make_async_remote_copy(
            src_ref=piece_ref,
            dst_ref=out_ref.at[me],
            send_sem=send_sem.at[k],
            recv_sem=recv_sem.at[k],
            device_id=device(lax.rem(me + k, n)),
            device_id_type=MESH,
        )
        copy.start()
        sends.append(copy)
    local.wait()
    for copy in sends:
        copy.wait_send()
    for k in range(1, n):
        source = lax.rem(me + n - k, n)
        pltpu.make_async_remote_copy(
            src_ref=piece_ref,
            dst_ref=out_ref.at[source],
            send_sem=send_sem.at[k],
            recv_sem=recv_sem.at[k],
            device_id=device(source),
            device_id_type=MESH,
        ).wait_recv()


def scatter_kernel(axis, other_axis, n, piece, keys_ref, values_ref, out_ref, send_sem, recv_sem, local_sem):
    me = lax.axis_index(axis)
    other = lax.axis_index(other_axis)

    def device(j):
        return (j, other) if axis == "ctx" else (other, j)

    def rows(j):
        return pl.ds(pl.multiple_of(j * piece, piece), piece)

    barrier = pltpu.get_barrier_semaphore()
    for k in range(1, n):
        pl.semaphore_signal(barrier, inc=1, device_id=device(lax.rem(me + k, n)), device_id_type=MESH)
    pl.semaphore_wait(barrier, n - 1)
    sources = (keys_ref, values_ref)
    local = [
        pltpu.make_async_copy(src.at[rows(me)], out_ref.at[me, t], local_sem.at[t])
        for t, src in enumerate(sources)
    ]
    for copy in local:
        copy.start()
    sends = []
    for k in range(1, n):
        peer = lax.rem(me + k, n)
        for t, src in enumerate(sources):
            copy = pltpu.make_async_remote_copy(
                src_ref=src.at[rows(peer)],
                dst_ref=out_ref.at[me, t],
                send_sem=send_sem.at[k, t],
                recv_sem=recv_sem.at[k, t],
                device_id=device(peer),
                device_id_type=MESH,
            )
            copy.start()
            sends.append(copy)
    for copy in local:
        copy.wait()
    for copy in sends:
        copy.wait_send()
    for k in range(1, n):
        source = lax.rem(me + n - k, n)
        for t, src in enumerate(sources):
            pltpu.make_async_remote_copy(
                src_ref=src.at[rows(me)],
                dst_ref=out_ref.at[source, t],
                send_sem=send_sem.at[k, t],
                recv_sem=recv_sem.at[k, t],
                device_id=device(source),
                device_id_type=MESH,
            ).wait_recv()


def scatter_bank(ref_keys, ref_values, axis, other_axis, n, collective_id):
    rows, width = ref_keys.shape
    piece = rows // n
    return pl.pallas_call(
        functools.partial(scatter_kernel, axis, other_axis, n, piece),
        out_shape=jax.ShapeDtypeStruct((n, 2, piece, width), ref_keys.dtype),
        in_specs=[pl.BlockSpec(memory_space=pl.ANY)] * 2,
        out_specs=pl.BlockSpec(memory_space=pl.ANY),
        scratch_shapes=[
            pltpu.SemaphoreType.DMA((n, 2)),
            pltpu.SemaphoreType.DMA((n, 2)),
            pltpu.SemaphoreType.DMA((2,)),
        ],
        compiler_params=pltpu.CompilerParams(collective_id=collective_id, has_side_effects=True),
    )(ref_keys, ref_values)


def gather_all(piece, axis, other_axis, n, collective_id):
    return pl.pallas_call(
        functools.partial(gather_kernel, axis, other_axis, n),
        out_shape=jax.ShapeDtypeStruct((n,) + piece.shape, piece.dtype),
        in_specs=[pl.BlockSpec(memory_space=pl.ANY)],
        out_specs=pl.BlockSpec(memory_space=pl.ANY),
        scratch_shapes=[
            pltpu.SemaphoreType.DMA((n,)),
            pltpu.SemaphoreType.DMA((n,)),
            pltpu.SemaphoreType.DMA(()),
        ],
        compiler_params=pltpu.CompilerParams(collective_id=collective_id, has_side_effects=True),
    )(piece)


def attend_kernel(
    label_ref, source_ref, q_ref, k_ref, v_ref, got_ref, whole_ref, w_hbm, o_ref, p_ref,
    far_k, far_v, bank_k, bank_v, w_vmem, sem_k, sem_v, sem_bank, sem_w,
):
    weight_copy = pltpu.make_async_copy(w_hbm, w_vmem, sem_w)
    weight_copy.start()
    n_blocks = far_k.shape[0]
    far_count = far_k.shape[1] // BLK
    piece = bank_k.shape[2]
    pending = []
    for position in range(n_blocks):
        person = label_ref[position]
        copies = []
        for j in range(far_count):
            source = source_ref[person * far_count + j]
            copies.append(pltpu.make_async_copy(
                got_ref.at[source, 0, pl.ds(0, BLK)], far_k.at[position, pl.ds(j * BLK, BLK)],
                sem_k.at[position, j]))
            copies.append(pltpu.make_async_copy(
                got_ref.at[source, 1, pl.ds(0, BLK)], far_v.at[position, pl.ds(j * BLK, BLK)],
                sem_v.at[position, j]))
        copies.append(pltpu.make_async_copy(
            whole_ref.at[:, pl.ds(person * 2 * piece, piece)], bank_k.at[position], sem_bank.at[position, 0]))
        copies.append(pltpu.make_async_copy(
            whole_ref.at[:, pl.ds(person * 2 * piece + piece, piece)], bank_v.at[position],
            sem_bank.at[position, 1]))
        for copy in copies:
            copy.start()
        pending.append(copies)
    width = q_ref.shape[1]
    bank_rows = bank_k.shape[1] * piece
    dims = (((1,), (1,)), ((), ()))
    for position in range(n_blocks):
        for copy in pending[position]:
            copy.wait()
        rows = pl.ds(position * BLK, BLK)
        for h in range(width // HD):
            cols = pl.ds(h * HD, HD)
            query = q_ref[rows, cols]
            parts = [
                (k_ref[rows, cols], v_ref[rows, cols]),
                (far_k[position, :, cols], far_v[position, :, cols]),
                (
                    bank_k[position, :, :, cols].reshape(bank_rows, HD),
                    bank_v[position, :, :, cols].reshape(bank_rows, HD),
                ),
            ]
            scores = [
                lax.dot_general(query, key, dims, preferred_element_type=jnp.float32) * HD ** (-0.5)
                for key, _ in parts
            ]
            peak = jnp.max(scores[0], axis=1, keepdims=True)
            for score in scores[1:]:
                peak = jnp.maximum(peak, jnp.max(score, axis=1, keepdims=True))
            total = None
            summed = None
            for score, (_, value) in zip(scores, parts):
                exponent = jnp.exp(score - peak)
                part_sum = jnp.sum(exponent, axis=1, keepdims=True)
                product = jnp.dot(exponent.astype(jnp.bfloat16), value, preferred_element_type=jnp.float32)
                total = part_sum if total is None else total + part_sum
                summed = product if summed is None else summed + product
            o_ref[rows, cols] = (summed / total).astype(o_ref.dtype)
    weight_copy.wait()
    mixed_in = o_ref[...]
    chunk = 512
    for j in range(p_ref.shape[1] // chunk):
        out_cols = pl.ds(j * chunk, chunk)
        p_ref[:, out_cols] = jnp.dot(
            mixed_in, w_vmem[:, out_cols], preferred_element_type=jnp.float32
        ).astype(p_ref.dtype)


def attend(labels, sources, q_norm, k_norm, values, got, whole, out_weight, n_ctx, far_count):
    rows, width = q_norm.shape
    n_blocks = rows // BLK
    piece = whole.shape[1] // 4
    vmem = pl.BlockSpec(memory_space=pltpu.VMEM)
    smem = pl.BlockSpec(memory_space=pltpu.SMEM)
    return pl.pallas_call(
        attend_kernel,
        out_shape=(
            jax.ShapeDtypeStruct((rows, width), jnp.bfloat16),
            jax.ShapeDtypeStruct((rows, out_weight.shape[1]), jnp.bfloat16),
        ),
        in_specs=[smem, smem, vmem, vmem, vmem] + [pl.BlockSpec(memory_space=pl.ANY)] * 3,
        out_specs=(vmem, vmem),
        scratch_shapes=[
            pltpu.VMEM((n_blocks, far_count * BLK, width), jnp.bfloat16),
            pltpu.VMEM((n_blocks, far_count * BLK, width), jnp.bfloat16),
            pltpu.VMEM((n_blocks, n_ctx, piece, width), jnp.bfloat16),
            pltpu.VMEM((n_blocks, n_ctx, piece, width), jnp.bfloat16),
            pltpu.VMEM(out_weight.shape, out_weight.dtype),
            pltpu.SemaphoreType.DMA((n_blocks, far_count)),
            pltpu.SemaphoreType.DMA((n_blocks, far_count)),
            pltpu.SemaphoreType.DMA((n_blocks, 2)),
            pltpu.SemaphoreType.DMA(()),
        ],
    )(labels, sources, q_norm, k_norm, values, got, whole, out_weight)


def normalize(features, scale_gain, square_total):
    factor = lax.rsqrt(square_total / D + epsilon)
    return (features * factor[:, None] * scale_gain[None, :]).astype(jnp.bfloat16)


def attend_block(query, own_keys, own_values, far_keys, far_values, bank_keys, bank_values):
    row_count, width = query.shape
    head_count = width // HD
    key_set = jnp.concatenate([own_keys, far_keys, bank_keys], axis=0)
    value_set = jnp.concatenate([own_values, far_values, bank_values], axis=0)
    query_heads = query.reshape(row_count, head_count, HD)
    key_heads = key_set.reshape(-1, head_count, HD)
    value_heads = value_set.reshape(-1, head_count, HD)
    scores = jnp.einsum(
        "qhd,khd->hqk", query_heads, key_heads, preferred_element_type=jnp.float32
    ) * HD ** (-0.5)
    row_peak = jnp.max(scores, axis=2, keepdims=True)
    exponent = jnp.exp(scores - row_peak)
    denominator = jnp.sum(exponent, axis=2)
    weights = exponent.astype(jnp.bfloat16)
    combined = jnp.einsum("hqk,khd->qhd", weights, value_heads, preferred_element_type=jnp.float32)
    return (combined / denominator.T[:, :, None]).reshape(row_count, width).astype(jnp.bfloat16)


def shards(
    queries,
    keys,
    values,
    q_gain,
    k_gain,
    ref_keys,
    ref_values,
    out_weight,
    partners,
    owners,
    labels,
):
    tokens, width = queries.shape
    blocks = tokens // BLK
    n_ctx = partners.shape[0]
    persons = partners.shape[1]
    bank_rows = ref_keys.shape[0]
    piece = bank_rows // n_ctx
    own_index = lax.axis_index("ctx")
    q_float = queries.astype(jnp.float32)
    k_float = keys.astype(jnp.float32)
    n_head = lax.axis_size("head")
    squares = jnp.stack([jnp.sum(q_float * q_float, axis=1), jnp.sum(k_float * k_float, axis=1)])
    q_total, k_total = jnp.sum(gather_all(squares, "head", "ctx", n_head, 1), axis=0)
    q_norm = normalize(q_float, q_gain, q_total)
    k_norm = normalize(k_float, k_gain, k_total)
    query_blocks = q_norm.reshape(blocks, BLK, width)
    key_blocks = k_norm.reshape(blocks, BLK, width)
    value_blocks = values.reshape(blocks, BLK, width)

    flat = partners.reshape(n_ctx, -1)
    hit = (flat // blocks) == own_index
    pick = jnp.sum(jnp.where(hit, flat % blocks, 0), axis=1)
    kv_blocks = jnp.stack([key_blocks, value_blocks], axis=1)
    send = kv_blocks[pick]
    got = lax.all_to_all(send, "ctx", 0, 0, tiled=True)
    bank = jnp.stack([ref_keys, ref_values]).reshape(2, n_ctx, piece, width)
    got_bank = lax.all_to_all(jnp.transpose(bank, (1, 0, 2, 3)), "ctx", 0, 0, tiled=True)

    sources = (partners[own_index] // blocks).reshape(-1)
    mine = got_bank[owners]
    piece_rows = mine.reshape(-1, width)
    whole = lax.all_to_all(
        jnp.broadcast_to(piece_rows, (n_ctx,) + piece_rows.shape), "ctx", 0, 0, tiled=True
    )
    attended, partial_out = attend(
        labels, sources, q_norm, k_norm, values, got, whole, out_weight, n_ctx, partners.shape[2]
    )
    mixed = lax.psum_scatter(partial_out, "head", scatter_dimension=1, tiled=True)
    return (attended, mixed)


def solution(mesh):
    return jax.shard_map(
        shards,
        mesh=mesh,
        in_specs=(
            P("ctx", "head"),
            P("ctx", "head"),
            P("ctx", "head"),
            P("head"),
            P("head"),
            P("ctx", "head"),
            P("ctx", "head"),
            P("head", None),
            P(),
            P(),
            P("ctx"),
        ),
        out_specs=(P("ctx", "head"), P("ctx", "head")),
        check_vma=False,
    )
```

```python
import functools

import jax
import jax.numpy as jnp
from jax import lax
from jax.experimental import pallas as pl
from jax.experimental.pallas import tpu as pltpu
from jax.sharding import PartitionSpec as P

MESH = pl.DeviceIdType.MESH

D = 5120
HD = 128
BLK = 128


epsilon = 1e-06


def gather_kernel(axis, other_axis, n, piece_ref, out_ref, send_sem, recv_sem, local_sem):
    me = lax.axis_index(axis)
    other = lax.axis_index(other_axis)

    def device(j):
        return (j, other) if axis == "ctx" else (other, j)

    barrier = pltpu.get_barrier_semaphore()
    for k in range(1, n):
        pl.semaphore_signal(barrier, inc=1, device_id=device(lax.rem(me + k, n)), device_id_type=MESH)
    pl.semaphore_wait(barrier, n - 1)
    local = pltpu.make_async_copy(piece_ref, out_ref.at[me], local_sem)
    local.start()
    sends = []
    for k in range(1, n):
        copy = pltpu.make_async_remote_copy(
            src_ref=piece_ref,
            dst_ref=out_ref.at[me],
            send_sem=send_sem.at[k],
            recv_sem=recv_sem.at[k],
            device_id=device(lax.rem(me + k, n)),
            device_id_type=MESH,
        )
        copy.start()
        sends.append(copy)
    local.wait()
    for copy in sends:
        copy.wait_send()
    for k in range(1, n):
        source = lax.rem(me + n - k, n)
        pltpu.make_async_remote_copy(
            src_ref=piece_ref,
            dst_ref=out_ref.at[source],
            send_sem=send_sem.at[k],
            recv_sem=recv_sem.at[k],
            device_id=device(source),
            device_id_type=MESH,
        ).wait_recv()


def scatter_kernel(axis, other_axis, n, piece, keys_ref, values_ref, out_ref, send_sem, recv_sem, local_sem):
    me = lax.axis_index(axis)
    other = lax.axis_index(other_axis)

    def device(j):
        return (j, other) if axis == "ctx" else (other, j)

    def rows(j):
        return pl.ds(pl.multiple_of(j * piece, piece), piece)

    barrier = pltpu.get_barrier_semaphore()
    for k in range(1, n):
        pl.semaphore_signal(barrier, inc=1, device_id=device(lax.rem(me + k, n)), device_id_type=MESH)
    pl.semaphore_wait(barrier, n - 1)
    sources = (keys_ref, values_ref)
    local = [
        pltpu.make_async_copy(src.at[rows(me)], out_ref.at[me, t], local_sem.at[t])
        for t, src in enumerate(sources)
    ]
    for copy in local:
        copy.start()
    sends = []
    for k in range(1, n):
        peer = lax.rem(me + k, n)
        for t, src in enumerate(sources):
            copy = pltpu.make_async_remote_copy(
                src_ref=src.at[rows(peer)],
                dst_ref=out_ref.at[me, t],
                send_sem=send_sem.at[k, t],
                recv_sem=recv_sem.at[k, t],
                device_id=device(peer),
                device_id_type=MESH,
            )
            copy.start()
            sends.append(copy)
    for copy in local:
        copy.wait()
    for copy in sends:
        copy.wait_send()
    for k in range(1, n):
        source = lax.rem(me + n - k, n)
        for t, src in enumerate(sources):
            pltpu.make_async_remote_copy(
                src_ref=src.at[rows(me)],
                dst_ref=out_ref.at[source, t],
                send_sem=send_sem.at[k, t],
                recv_sem=recv_sem.at[k, t],
                device_id=device(source),
                device_id_type=MESH,
            ).wait_recv()


def scatter_bank(ref_keys, ref_values, axis, other_axis, n, collective_id):
    rows, width = ref_keys.shape
    piece = rows // n
    return pl.pallas_call(
        functools.partial(scatter_kernel, axis, other_axis, n, piece),
        out_shape=jax.ShapeDtypeStruct((n, 2, piece, width), ref_keys.dtype),
        in_specs=[pl.BlockSpec(memory_space=pl.ANY)] * 2,
        out_specs=pl.BlockSpec(memory_space=pl.ANY),
        scratch_shapes=[
            pltpu.SemaphoreType.DMA((n, 2)),
            pltpu.SemaphoreType.DMA((n, 2)),
            pltpu.SemaphoreType.DMA((2,)),
        ],
        compiler_params=pltpu.CompilerParams(collective_id=collective_id, has_side_effects=True),
    )(ref_keys, ref_values)


def gather_all(piece, axis, other_axis, n, collective_id):
    return pl.pallas_call(
        functools.partial(gather_kernel, axis, other_axis, n),
        out_shape=jax.ShapeDtypeStruct((n,) + piece.shape, piece.dtype),
        in_specs=[pl.BlockSpec(memory_space=pl.ANY)],
        out_specs=pl.BlockSpec(memory_space=pl.ANY),
        scratch_shapes=[
            pltpu.SemaphoreType.DMA((n,)),
            pltpu.SemaphoreType.DMA((n,)),
            pltpu.SemaphoreType.DMA(()),
        ],
        compiler_params=pltpu.CompilerParams(collective_id=collective_id, has_side_effects=True),
    )(piece)


def attend_kernel(
    label_ref, source_ref, q_ref, k_ref, v_ref, got_ref, whole_ref, w_hbm, o_ref, p_ref,
    far_k, far_v, bank_k, bank_v, w_vmem, sem_k, sem_v, sem_bank, sem_w,
):
    weight_copy = pltpu.make_async_copy(w_hbm, w_vmem, sem_w)
    weight_copy.start()
    n_blocks = far_k.shape[0]
    far_count = far_k.shape[1] // BLK
    piece = bank_k.shape[2]
    pending = []
    for position in range(n_blocks):
        person = label_ref[position]
        copies = []
        for j in range(far_count):
            source = source_ref[person * far_count + j]
            copies.append(pltpu.make_async_copy(
                got_ref.at[source, 0, pl.ds(0, BLK)], far_k.at[position, pl.ds(j * BLK, BLK)],
                sem_k.at[position, j]))
            copies.append(pltpu.make_async_copy(
                got_ref.at[source, 1, pl.ds(0, BLK)], far_v.at[position, pl.ds(j * BLK, BLK)],
                sem_v.at[position, j]))
        copies.append(pltpu.make_async_copy(
            whole_ref.at[:, pl.ds(person * 2 * piece, piece)], bank_k.at[position], sem_bank.at[position, 0]))
        copies.append(pltpu.make_async_copy(
            whole_ref.at[:, pl.ds(person * 2 * piece + piece, piece)], bank_v.at[position],
            sem_bank.at[position, 1]))
        for copy in copies:
            copy.start()
        pending.append(copies)
    width = q_ref.shape[1]
    bank_rows = bank_k.shape[1] * piece
    dims = (((1,), (1,)), ((), ()))
    for position in range(n_blocks):
        for copy in pending[position]:
            copy.wait()
        rows = pl.ds(position * BLK, BLK)
        for h in range(width // HD):
            cols = pl.ds(h * HD, HD)
            query = q_ref[rows, cols]
            parts = [
                (k_ref[rows, cols], v_ref[rows, cols]),
                (far_k[position, :, cols], far_v[position, :, cols]),
                (
                    bank_k[position, :, :, cols].reshape(bank_rows, HD),
                    bank_v[position, :, :, cols].reshape(bank_rows, HD),
                ),
            ]
            scores = [
                lax.dot_general(query, key, dims, preferred_element_type=jnp.float32) * HD ** (-0.5)
                for key, _ in parts
            ]
            peak = jnp.max(scores[0], axis=1, keepdims=True)
            for score in scores[1:]:
                peak = jnp.maximum(peak, jnp.max(score, axis=1, keepdims=True))
            total = None
            summed = None
            for score, (_, value) in zip(scores, parts):
                exponent = jnp.exp(score - peak)
                part_sum = jnp.sum(exponent, axis=1, keepdims=True)
                product = jnp.dot(exponent.astype(jnp.bfloat16), value, preferred_element_type=jnp.float32)
                total = part_sum if total is None else total + part_sum
                summed = product if summed is None else summed + product
            o_ref[rows, cols] = (summed / total).astype(o_ref.dtype)
    weight_copy.wait()
    mixed_in = o_ref[...]
    chunk = 512
    for j in range(p_ref.shape[0] // chunk):
        out_cols = pl.ds(j * chunk, chunk)
        p_ref[out_cols, :] = jnp.dot(
            mixed_in, w_vmem[:, out_cols], preferred_element_type=jnp.float32
        ).T.astype(p_ref.dtype)


def attend(labels, sources, q_norm, k_norm, values, got, whole, out_weight, n_ctx, far_count):
    rows, width = q_norm.shape
    n_blocks = rows // BLK
    piece = whole.shape[1] // 4
    vmem = pl.BlockSpec(memory_space=pltpu.VMEM)
    smem = pl.BlockSpec(memory_space=pltpu.SMEM)
    return pl.pallas_call(
        attend_kernel,
        out_shape=(
            jax.ShapeDtypeStruct((rows, width), jnp.bfloat16),
            jax.ShapeDtypeStruct((out_weight.shape[1], rows), jnp.bfloat16),
        ),
        in_specs=[smem, smem, vmem, vmem, vmem] + [pl.BlockSpec(memory_space=pl.ANY)] * 3,
        out_specs=(vmem, vmem),
        scratch_shapes=[
            pltpu.VMEM((n_blocks, far_count * BLK, width), jnp.bfloat16),
            pltpu.VMEM((n_blocks, far_count * BLK, width), jnp.bfloat16),
            pltpu.VMEM((n_blocks, n_ctx, piece, width), jnp.bfloat16),
            pltpu.VMEM((n_blocks, n_ctx, piece, width), jnp.bfloat16),
            pltpu.VMEM(out_weight.shape, out_weight.dtype),
            pltpu.SemaphoreType.DMA((n_blocks, far_count)),
            pltpu.SemaphoreType.DMA((n_blocks, far_count)),
            pltpu.SemaphoreType.DMA((n_blocks, 2)),
            pltpu.SemaphoreType.DMA(()),
        ],
    )(labels, sources, q_norm, k_norm, values, got, whole, out_weight)


def normalize(features, scale_gain, square_total):
    factor = lax.rsqrt(square_total / D + epsilon)
    return (features * factor[:, None] * scale_gain[None, :]).astype(jnp.bfloat16)


def attend_block(query, own_keys, own_values, far_keys, far_values, bank_keys, bank_values):
    row_count, width = query.shape
    head_count = width // HD
    key_set = jnp.concatenate([own_keys, far_keys, bank_keys], axis=0)
    value_set = jnp.concatenate([own_values, far_values, bank_values], axis=0)
    query_heads = query.reshape(row_count, head_count, HD)
    key_heads = key_set.reshape(-1, head_count, HD)
    value_heads = value_set.reshape(-1, head_count, HD)
    scores = jnp.einsum(
        "qhd,khd->hqk", query_heads, key_heads, preferred_element_type=jnp.float32
    ) * HD ** (-0.5)
    row_peak = jnp.max(scores, axis=2, keepdims=True)
    exponent = jnp.exp(scores - row_peak)
    denominator = jnp.sum(exponent, axis=2)
    weights = exponent.astype(jnp.bfloat16)
    combined = jnp.einsum("hqk,khd->qhd", weights, value_heads, preferred_element_type=jnp.float32)
    return (combined / denominator.T[:, :, None]).reshape(row_count, width).astype(jnp.bfloat16)


def shards(
    queries,
    keys,
    values,
    q_gain,
    k_gain,
    ref_keys,
    ref_values,
    out_weight,
    partners,
    owners,
    labels,
):
    tokens, width = queries.shape
    blocks = tokens // BLK
    n_ctx = partners.shape[0]
    persons = partners.shape[1]
    bank_rows = ref_keys.shape[0]
    piece = bank_rows // n_ctx
    own_index = lax.axis_index("ctx")
    q_float = queries.astype(jnp.float32)
    k_float = keys.astype(jnp.float32)
    n_head = lax.axis_size("head")
    squares = jnp.stack([jnp.sum(q_float * q_float, axis=1), jnp.sum(k_float * k_float, axis=1)])
    q_total, k_total = jnp.sum(gather_all(squares, "head", "ctx", n_head, 1), axis=0)
    q_norm = normalize(q_float, q_gain, q_total)
    k_norm = normalize(k_float, k_gain, k_total)
    query_blocks = q_norm.reshape(blocks, BLK, width)
    key_blocks = k_norm.reshape(blocks, BLK, width)
    value_blocks = values.reshape(blocks, BLK, width)

    flat = partners.reshape(n_ctx, -1)
    hit = (flat // blocks) == own_index
    pick = jnp.sum(jnp.where(hit, flat % blocks, 0), axis=1)
    kv_blocks = jnp.stack([key_blocks, value_blocks], axis=1)
    send = kv_blocks[pick]
    got = lax.all_to_all(send, "ctx", 0, 0, tiled=True)
    bank = jnp.stack([ref_keys, ref_values]).reshape(2, n_ctx, piece, width)
    got_bank = lax.all_to_all(jnp.transpose(bank, (1, 0, 2, 3)), "ctx", 0, 0, tiled=True)

    sources = (partners[own_index] // blocks).reshape(-1)
    mine = got_bank[owners]
    piece_rows = mine.reshape(-1, width)
    whole = lax.all_to_all(
        jnp.broadcast_to(piece_rows, (n_ctx,) + piece_rows.shape), "ctx", 0, 0, tiled=True
    )
    attended, partial_out = attend(
        labels, sources, q_norm, k_norm, values, got, whole, out_weight, n_ctx, partners.shape[2]
    )
    mixed = lax.psum_scatter(partial_out, "head", scatter_dimension=0, tiled=True).T
    return (attended, mixed)


def solution(mesh):
    return jax.shard_map(
        shards,
        mesh=mesh,
        in_specs=(
            P("ctx", "head"),
            P("ctx", "head"),
            P("ctx", "head"),
            P("head"),
            P("head"),
            P("ctx", "head"),
            P("ctx", "head"),
            P("head", None),
            P(),
            P(),
            P("ctx"),
        ),
        out_specs=(P("ctx", "head"), P("ctx", "head")),
        check_vma=False,
    )
```

```python
import functools

import jax
import jax.numpy as jnp
from jax import lax
from jax.experimental import pallas as pl
from jax.experimental.pallas import tpu as pltpu
from jax.sharding import PartitionSpec as P

MESH = pl.DeviceIdType.MESH

D = 5120
HD = 128
BLK = 128


epsilon = 1e-06


def gather_kernel(axis, other_axis, n, piece_ref, out_ref, send_sem, recv_sem, local_sem):
    me = lax.axis_index(axis)
    other = lax.axis_index(other_axis)

    def device(j):
        return (j, other) if axis == "ctx" else (other, j)

    barrier = pltpu.get_barrier_semaphore()
    for k in range(1, n):
        pl.semaphore_signal(barrier, inc=1, device_id=device(lax.rem(me + k, n)), device_id_type=MESH)
    pl.semaphore_wait(barrier, n - 1)
    local = pltpu.make_async_copy(piece_ref, out_ref.at[me], local_sem)
    local.start()
    sends = []
    for k in range(1, n):
        copy = pltpu.make_async_remote_copy(
            src_ref=piece_ref,
            dst_ref=out_ref.at[me],
            send_sem=send_sem.at[k],
            recv_sem=recv_sem.at[k],
            device_id=device(lax.rem(me + k, n)),
            device_id_type=MESH,
        )
        copy.start()
        sends.append(copy)
    local.wait()
    for copy in sends:
        copy.wait_send()
    for k in range(1, n):
        source = lax.rem(me + n - k, n)
        pltpu.make_async_remote_copy(
            src_ref=piece_ref,
            dst_ref=out_ref.at[source],
            send_sem=send_sem.at[k],
            recv_sem=recv_sem.at[k],
            device_id=device(source),
            device_id_type=MESH,
        ).wait_recv()


def scatter_kernel(axis, other_axis, n, piece, keys_ref, values_ref, out_ref, send_sem, recv_sem, local_sem):
    me = lax.axis_index(axis)
    other = lax.axis_index(other_axis)

    def device(j):
        return (j, other) if axis == "ctx" else (other, j)

    def rows(j):
        return pl.ds(pl.multiple_of(j * piece, piece), piece)

    barrier = pltpu.get_barrier_semaphore()
    for k in range(1, n):
        pl.semaphore_signal(barrier, inc=1, device_id=device(lax.rem(me + k, n)), device_id_type=MESH)
    pl.semaphore_wait(barrier, n - 1)
    sources = (keys_ref, values_ref)
    local = [
        pltpu.make_async_copy(src.at[rows(me)], out_ref.at[me, t], local_sem.at[t])
        for t, src in enumerate(sources)
    ]
    for copy in local:
        copy.start()
    sends = []
    for k in range(1, n):
        peer = lax.rem(me + k, n)
        for t, src in enumerate(sources):
            copy = pltpu.make_async_remote_copy(
                src_ref=src.at[rows(peer)],
                dst_ref=out_ref.at[me, t],
                send_sem=send_sem.at[k, t],
                recv_sem=recv_sem.at[k, t],
                device_id=device(peer),
                device_id_type=MESH,
            )
            copy.start()
            sends.append(copy)
    for copy in local:
        copy.wait()
    for copy in sends:
        copy.wait_send()
    for k in range(1, n):
        source = lax.rem(me + n - k, n)
        for t, src in enumerate(sources):
            pltpu.make_async_remote_copy(
                src_ref=src.at[rows(me)],
                dst_ref=out_ref.at[source, t],
                send_sem=send_sem.at[k, t],
                recv_sem=recv_sem.at[k, t],
                device_id=device(source),
                device_id_type=MESH,
            ).wait_recv()


def scatter_bank(ref_keys, ref_values, axis, other_axis, n, collective_id):
    rows, width = ref_keys.shape
    piece = rows // n
    return pl.pallas_call(
        functools.partial(scatter_kernel, axis, other_axis, n, piece),
        out_shape=jax.ShapeDtypeStruct((n, 2, piece, width), ref_keys.dtype),
        in_specs=[pl.BlockSpec(memory_space=pl.ANY)] * 2,
        out_specs=pl.BlockSpec(memory_space=pl.ANY),
        scratch_shapes=[
            pltpu.SemaphoreType.DMA((n, 2)),
            pltpu.SemaphoreType.DMA((n, 2)),
            pltpu.SemaphoreType.DMA((2,)),
        ],
        compiler_params=pltpu.CompilerParams(collective_id=collective_id, has_side_effects=True),
    )(ref_keys, ref_values)


def gather_all(piece, axis, other_axis, n, collective_id):
    return pl.pallas_call(
        functools.partial(gather_kernel, axis, other_axis, n),
        out_shape=jax.ShapeDtypeStruct((n,) + piece.shape, piece.dtype),
        in_specs=[pl.BlockSpec(memory_space=pl.ANY)],
        out_specs=pl.BlockSpec(memory_space=pl.ANY),
        scratch_shapes=[
            pltpu.SemaphoreType.DMA((n,)),
            pltpu.SemaphoreType.DMA((n,)),
            pltpu.SemaphoreType.DMA(()),
        ],
        compiler_params=pltpu.CompilerParams(collective_id=collective_id, has_side_effects=True),
    )(piece)


def attend_kernel(
    label_ref, source_ref, q_ref, k_ref, v_ref, got_ref, whole_ref, w_hbm, o_ref, p_ref,
    far_k, far_v, bank_k, bank_v, w_vmem, sem_k, sem_v, sem_bank, sem_w,
):

    n_blocks = far_k.shape[0]
    far_count = far_k.shape[1] // BLK
    piece = bank_k.shape[2]
    pending = []
    for position in range(n_blocks):
        person = label_ref[position]
        copies = []
        for j in range(far_count):
            source = source_ref[person * far_count + j]
            copies.append(pltpu.make_async_copy(
                got_ref.at[source, 0, pl.ds(0, BLK)], far_k.at[position, pl.ds(j * BLK, BLK)],
                sem_k.at[position, j]))
            copies.append(pltpu.make_async_copy(
                got_ref.at[source, 1, pl.ds(0, BLK)], far_v.at[position, pl.ds(j * BLK, BLK)],
                sem_v.at[position, j]))
        copies.append(pltpu.make_async_copy(
            whole_ref.at[:, pl.ds(person * 2 * piece, piece)], bank_k.at[position], sem_bank.at[position, 0]))
        copies.append(pltpu.make_async_copy(
            whole_ref.at[:, pl.ds(person * 2 * piece + piece, piece)], bank_v.at[position],
            sem_bank.at[position, 1]))
        for copy in copies:
            copy.start()
        pending.append(copies)
    weight_copy = pltpu.make_async_copy(w_hbm, w_vmem, sem_w)
    weight_copy.start()
    width = q_ref.shape[1]
    bank_rows = bank_k.shape[1] * piece
    dims = (((1,), (1,)), ((), ()))
    for position in range(n_blocks):
        for copy in pending[position]:
            copy.wait()
        rows = pl.ds(position * BLK, BLK)
        for h in range(width // HD):
            cols = pl.ds(h * HD, HD)
            query = q_ref[rows, cols]
            parts = [
                (k_ref[rows, cols], v_ref[rows, cols]),
                (far_k[position, :, cols], far_v[position, :, cols]),
                (
                    bank_k[position, :, :, cols].reshape(bank_rows, HD),
                    bank_v[position, :, :, cols].reshape(bank_rows, HD),
                ),
            ]
            scores = [
                lax.dot_general(query, key, dims, preferred_element_type=jnp.float32) * HD ** (-0.5)
                for key, _ in parts
            ]
            peak = jnp.max(scores[0], axis=1, keepdims=True)
            for score in scores[1:]:
                peak = jnp.maximum(peak, jnp.max(score, axis=1, keepdims=True))
            total = None
            summed = None
            for score, (_, value) in zip(scores, parts):
                exponent = jnp.exp(score - peak)
                part_sum = jnp.sum(exponent, axis=1, keepdims=True)
                product = jnp.dot(exponent.astype(jnp.bfloat16), value, preferred_element_type=jnp.float32)
                total = part_sum if total is None else total + part_sum
                summed = product if summed is None else summed + product
            o_ref[rows, cols] = (summed / total).astype(o_ref.dtype)
    weight_copy.wait()
    mixed_in = o_ref[...]
    chunk = 512
    for j in range(p_ref.shape[0] // chunk):
        out_cols = pl.ds(j * chunk, chunk)
        p_ref[out_cols, :] = jnp.dot(
            mixed_in, w_vmem[:, out_cols], preferred_element_type=jnp.float32
        ).T.astype(p_ref.dtype)


def attend(labels, sources, q_norm, k_norm, values, got, whole, out_weight, n_ctx, far_count):
    rows, width = q_norm.shape
    n_blocks = rows // BLK
    piece = whole.shape[1] // 4
    vmem = pl.BlockSpec(memory_space=pltpu.VMEM)
    smem = pl.BlockSpec(memory_space=pltpu.SMEM)
    return pl.pallas_call(
        attend_kernel,
        out_shape=(
            jax.ShapeDtypeStruct((rows, width), jnp.bfloat16),
            jax.ShapeDtypeStruct((out_weight.shape[1], rows), jnp.bfloat16),
        ),
        in_specs=[smem, smem, vmem, vmem, vmem] + [pl.BlockSpec(memory_space=pl.ANY)] * 3,
        out_specs=(vmem, vmem),
        scratch_shapes=[
            pltpu.VMEM((n_blocks, far_count * BLK, width), jnp.bfloat16),
            pltpu.VMEM((n_blocks, far_count * BLK, width), jnp.bfloat16),
            pltpu.VMEM((n_blocks, n_ctx, piece, width), jnp.bfloat16),
            pltpu.VMEM((n_blocks, n_ctx, piece, width), jnp.bfloat16),
            pltpu.VMEM(out_weight.shape, out_weight.dtype),
            pltpu.SemaphoreType.DMA((n_blocks, far_count)),
            pltpu.SemaphoreType.DMA((n_blocks, far_count)),
            pltpu.SemaphoreType.DMA((n_blocks, 2)),
            pltpu.SemaphoreType.DMA(()),
        ],
    )(labels, sources, q_norm, k_norm, values, got, whole, out_weight)


def normalize(features, scale_gain, square_total):
    factor = lax.rsqrt(square_total / D + epsilon)
    return (features * factor[:, None] * scale_gain[None, :]).astype(jnp.bfloat16)


def attend_block(query, own_keys, own_values, far_keys, far_values, bank_keys, bank_values):
    row_count, width = query.shape
    head_count = width // HD
    key_set = jnp.concatenate([own_keys, far_keys, bank_keys], axis=0)
    value_set = jnp.concatenate([own_values, far_values, bank_values], axis=0)
    query_heads = query.reshape(row_count, head_count, HD)
    key_heads = key_set.reshape(-1, head_count, HD)
    value_heads = value_set.reshape(-1, head_count, HD)
    scores = jnp.einsum(
        "qhd,khd->hqk", query_heads, key_heads, preferred_element_type=jnp.float32
    ) * HD ** (-0.5)
    row_peak = jnp.max(scores, axis=2, keepdims=True)
    exponent = jnp.exp(scores - row_peak)
    denominator = jnp.sum(exponent, axis=2)
    weights = exponent.astype(jnp.bfloat16)
    combined = jnp.einsum("hqk,khd->qhd", weights, value_heads, preferred_element_type=jnp.float32)
    return (combined / denominator.T[:, :, None]).reshape(row_count, width).astype(jnp.bfloat16)


def shards(
    queries,
    keys,
    values,
    q_gain,
    k_gain,
    ref_keys,
    ref_values,
    out_weight,
    partners,
    owners,
    labels,
):
    tokens, width = queries.shape
    blocks = tokens // BLK
    n_ctx = partners.shape[0]
    persons = partners.shape[1]
    bank_rows = ref_keys.shape[0]
    piece = bank_rows // n_ctx
    own_index = lax.axis_index("ctx")
    q_float = queries.astype(jnp.float32)
    k_float = keys.astype(jnp.float32)
    n_head = lax.axis_size("head")
    squares = jnp.stack([jnp.sum(q_float * q_float, axis=1), jnp.sum(k_float * k_float, axis=1)])
    q_total, k_total = jnp.sum(gather_all(squares, "head", "ctx", n_head, 1), axis=0)
    q_norm = normalize(q_float, q_gain, q_total)
    k_norm = normalize(k_float, k_gain, k_total)
    query_blocks = q_norm.reshape(blocks, BLK, width)
    key_blocks = k_norm.reshape(blocks, BLK, width)
    value_blocks = values.reshape(blocks, BLK, width)

    flat = partners.reshape(n_ctx, -1)
    hit = (flat // blocks) == own_index
    pick = jnp.sum(jnp.where(hit, flat % blocks, 0), axis=1)
    kv_blocks = jnp.stack([key_blocks, value_blocks], axis=1)
    send = kv_blocks[pick]
    got = lax.all_to_all(send, "ctx", 0, 0, tiled=True)
    bank = jnp.stack([ref_keys, ref_values]).reshape(2, n_ctx, piece, width)
    got_bank = lax.all_to_all(jnp.transpose(bank, (1, 0, 2, 3)), "ctx", 0, 0, tiled=True)

    sources = (partners[own_index] // blocks).reshape(-1)
    mine = got_bank[owners]
    piece_rows = mine.reshape(-1, width)
    whole = lax.all_to_all(
        jnp.broadcast_to(piece_rows, (n_ctx,) + piece_rows.shape), "ctx", 0, 0, tiled=True
    )
    attended, partial_out = attend(
        labels, sources, q_norm, k_norm, values, got, whole, out_weight, n_ctx, partners.shape[2]
    )
    mixed = lax.psum_scatter(partial_out, "head", scatter_dimension=0, tiled=True).T
    return (attended, mixed)


def solution(mesh):
    return jax.shard_map(
        shards,
        mesh=mesh,
        in_specs=(
            P("ctx", "head"),
            P("ctx", "head"),
            P("ctx", "head"),
            P("head"),
            P("head"),
            P("ctx", "head"),
            P("ctx", "head"),
            P("head", None),
            P(),
            P(),
            P("ctx"),
        ),
        out_specs=(P("ctx", "head"), P("ctx", "head")),
        check_vma=False,
    )
```
